32 devices in a mesh: dom: 4 (over y, x), fsdp: 8 (over z, core).
Axes of the slice: x: 2, y: 2, z: 4, core: 2. Of those that a mesh axis runs over, the one named last changes fastest.
Arguments:
- inputs: bfloat16 [4, 1024, 4096], P('dom', 'fsdp'), may hold values from -6 to 6
- cotangent: bfloat16 [4, 1024, 8192], P('dom', 'fsdp'), may hold values from -6 to 6
- shared_weight: bfloat16 [4096, 8192], P(None, 'fsdp'), may hold values from -0.09375 to 0.09375
- domain_weight: bfloat16 [4, 4096, 8192], P('dom', None, 'fsdp'), may hold values from 0.099609375 to 1.8984375
- row_counts: int32 [4], P('dom'), may hold values from 65 to 1024, as said below
Outputs:
- shared_grad: float32 [4096, 8192], P('dom', 'fsdp')
- domain_grad: bfloat16 [4, 4096, 8192], P('dom', None, 'fsdp')
- input_grad: bfloat16 [4, 1024, 4096], P('dom', 'fsdp')
The draws below stay inside these ranges and needn't reach their ends.
Inputs may be any that keep to these rules, and one draw needn't show every extreme that they name: `row_counts`: rows of a domain at positions from its count on are padding. Some domain is full in every draw.
All inputs are finite; a program needn't handle non-finite values.
Results may differ from the reference program's by a relative error of at most 0.017.
Values may be sent and summed in bfloat16 or wider, within the bound.
A program may use at most 128 MiB of HBM per device.

```python
import jax
import jax.numpy as jnp
from jax import lax

D = 4096
H = 8192
DOMS = 4
CAP = 1024
N_FSDP = 8


def draw_row_counts(key, part):
    first, second, third = jax.random.split(jax.random.fold_in(key, 7), 3)
    shifts = jax.random.randint(first, (DOMS,), 0, 4)
    base = CAP // jnp.left_shift(jnp.int32(1), shifts.astype(jnp.int32))
    jitter = jax.random.randint(second, (DOMS,), 0, 1 << 30) % (base // 2)
    counts = base - jitter
    fuller = jax.random.randint(third, (), 0, DOMS)
    counts = jnp.where(jnp.arange(DOMS) == fuller, CAP, counts)
    return counts.astype(jnp.int32)


def shard_levels(stream_key, dims, pieces, smallest, top_value):
    gain = 1.0
    for axis_at, shards_of in pieces:
        heights = jax.random.uniform(jax.random.fold_in(jax.random.fold_in(stream_key, 6), axis_at), (shards_of,), jnp.float32, smallest / len(pieces), top_value / len(pieces))
        gain = gain * jnp.repeat(jnp.exp(heights), dims[axis_at] // shards_of).reshape((-1,) + (1,) * (len(dims) - 1 - axis_at))
    return gain


def gaussian(rng, extent, spread, bound, cuts=(), held_as=jnp.bfloat16):
    loudness = shard_levels(rng, extent, cuts, -0.22, 0.18) if cuts else 1.0
    result = jax.random.normal(rng, extent, jnp.float32) * spread * loudness
    return jnp.minimum(jnp.maximum(result, -bound), bound).astype(held_as)


def setup_inputs(seed: int = 0) -> dict:
    keys = jax.random.split(jax.random.key(seed), 6)
    return {
        "inputs": gaussian(keys[0], (DOMS, CAP, D), 1.0, 6.0, ((0, 4), (1, 8))),
        "cotangent": gaussian(keys[1], (DOMS, CAP, H), 1.0, 6.0, ((0, 4), (1, 8))),
        "shared_weight": gaussian(keys[2], (D, H), D ** -0.5, 0.09375, ((1, 8),)),
        "domain_weight": jnp.clip(1.0 + 0.18 * jax.random.normal(keys[3], (DOMS, D, H), jnp.float32), 0.099609375, 1.8984375).astype(jnp.bfloat16),
        "row_counts": draw_row_counts(jax.random.fold_in(keys[5], 71), 0),
    }


def domain_pass(shared_weight, inputs_g, upstream_g, weight_g, count_g):
    effective = (shared_weight.astype(jnp.float32) * weight_g.astype(jnp.float32)).astype(jnp.bfloat16)
    preact = jnp.dot(inputs_g, effective, preferred_element_type=jnp.float32)
    sigma = jax.nn.sigmoid(preact)
    position = jnp.arange(CAP, dtype=jnp.int32)
    live = (position < count_g)[:, None]
    slope = upstream_g.astype(jnp.float32) * sigma * (1.0 + preact * (1.0 - sigma))
    grad_pre = jnp.where(live, slope, jnp.float32(0.0)).astype(jnp.bfloat16)
    scale = lax.rsqrt(count_g.astype(jnp.float32))
    weight_sum = jnp.dot(inputs_g.T, grad_pre, preferred_element_type=jnp.float32) * scale
    shared_term = weight_sum * weight_g.astype(jnp.float32)
    domain_grad = (weight_sum * shared_weight.astype(jnp.float32)).astype(jnp.bfloat16)
    width = H // N_FSDP

    def add_block(total, block):
        start = (block * width).astype(jnp.int32)
        grad_cols = lax.dynamic_slice_in_dim(grad_pre, start, width, 1)
        eff_cols = lax.dynamic_slice_in_dim(effective, start, width, 1)
        partial_sum = jnp.dot(grad_cols, eff_cols.T, preferred_element_type=jnp.float32)
        rounded = lax.optimization_barrier(partial_sum.astype(jnp.bfloat16))
        return (total + rounded.astype(jnp.float32), None)
    total, _ = lax.scan(add_block, jnp.zeros((CAP, D), jnp.float32), jnp.arange(N_FSDP, dtype=jnp.int32))
    return (shared_term, domain_grad, total.astype(jnp.bfloat16))

def reference(inputs, cotangent, shared_weight, domain_weight, row_counts):

    def step(carry, items):
        inputs_g, upstream_g, weight_g, count_g = items
        shared_term, domain_grad, input_grad = domain_pass(shared_weight, inputs_g, upstream_g, weight_g, count_g)
        return (carry + shared_term, (domain_grad, input_grad))
    shared_grad, outputs = lax.scan(step, jnp.zeros((D, H), jnp.float32), (inputs, cotangent, domain_weight, row_counts))
    return (shared_grad, outputs[0], outputs[1])
```

```python
import functools

import jax
import jax.numpy as jnp
from jax import lax
from jax.experimental import pallas as pl
from jax.experimental.pallas import tpu as pltpu
from jax.sharding import PartitionSpec as P

MESH = pl.DeviceIdType.MESH
F32 = jnp.float32
BF16 = jnp.bfloat16
CHUNKS = 4
PIECES = 8
PAIR = 2
HALVES = 2
TILE = 256


def fused_kernel(
    n, nd, x_ref, g_ref, sw_ref, dw_ref, count_ref, shared_out, dom_out, in_out,
    xs, gs, weff, tb, rb, sib, chain, dxb, swb, shv,
    up_sem, down_sem, side_sem, x_sem, gsend_sem, g_sem, own_sem, sw_sem, dw_sem,
    sib_send, sib_recv, ch_send, ch_recv, d_send, d_recv, dom_sem, out_sem, in_sem, ready,
):
    me, dom = lax.axis_index("fsdp"), lax.axis_index("dom")
    nz = n // 2
    z, c = lax.div(me, 2), lax.rem(me, 2)
    up, down, sibling = me + 2, me - 2, z * 2 + (1 - c)
    rows, depth = x_ref.shape
    width = sw_ref.shape[1]
    cw = width // CHUNKS
    pw = depth // PIECES
    block = depth // nd
    bits = nd.bit_length() - 1
    parts = min(2, bits)
    tile = min(TILE, block // parts)
    pieces = block // tile

    def flip(value, mask):
        for b in range(bits):
            if mask >> b & 1:
                value = value + (1 << b) - (2 << b) * lax.rem(lax.div(value, 1 << b), 2)
        return value

    barrier = pltpu.get_barrier_semaphore()

    def greet(k, carry):
        pl.semaphore_signal(
            barrier, inc=1, device_id={"fsdp": lax.rem(me + k, n)}, device_id_type=MESH
        )
        return carry

    lax.fori_loop(1, n, greet, 0)
    for b in range(bits):
        pl.semaphore_signal(
            barrier, inc=1, device_id={"dom": flip(dom, 1 << b)}, device_id_type=MESH
        )

    def cols(j):
        return pl.ds(pl.multiple_of(j * cw, cw), cw)

    def depth_cols(pc):
        return pl.ds(pl.multiple_of(pc * pw, pw), pw)

    def chip_rows(chip):
        return pl.ds(pl.multiple_of(chip * (2 * rows), 2 * rows), 2 * rows)

    def core_rows(chip, core):
        return pl.ds(pl.multiple_of((chip * 2 + core) * rows, rows), rows)

    def sw_load(j):
        return pltpu.make_async_copy(sw_ref.at[:, cols(j)], swb.at[lax.rem(j, 2)], sw_sem.at[j])

    def dw_load(j):
        return pltpu.make_async_copy(dw_ref.at[:, cols(j)], tb.at[j], dw_sem.at[j])

    own_x = pltpu.make_async_copy(x_ref, xs.at[core_rows(z, c)], own_sem.at[0])
    own_g = pltpu.make_async_copy(
        g_ref.at[:, pl.ds(pl.multiple_of(me * width, width), width)],
        gs.at[core_rows(z, c)],
        own_sem.at[1],
    )
    for j in range(CHUNKS):
        if j < 2:
            sw_load(j).start()
        dw_load(j).start()
    own_x.start()
    own_g.start()

    pl.semaphore_wait(barrier, n - 1 + bits)

    part = rows // HALVES

    def x_slot(chip, core, h):
        at = (chip * 2 + core) * rows + h * part
        return xs.at[pl.ds(pl.multiple_of(at, part), part)]

    def x_copy(src, chip, core, h, sem, target):
        return pltpu.make_async_remote_copy(
            src_ref=src,
            dst_ref=x_slot(chip, core, h),
            send_sem=sem.at[chip, h],
            recv_sem=x_sem.at[chip * 2 + core, h],
            device_id={"fsdp": target},
            device_id_type=MESH,
        )

    def g_copy(target, j):
        at = pl.ds(pl.multiple_of(target * width + j * cw, cw), cw)
        return pltpu.make_async_remote_copy(
            src_ref=g_ref.at[:, at],
            dst_ref=gs.at[core_rows(z, c), cols(j)],
            send_sem=gsend_sem.at[target, j],
            recv_sem=g_sem.at[me, j],
            device_id={"fsdp": target},
            device_id_type=MESH,
        )

    for h in range(HALVES):
        mine = x_ref.at[pl.ds(h * part, part)]

        @pl.when(z + 1 < nz)
        def _():
            x_copy(mine, z, c, h, up_sem, up).start()

        @pl.when(z > 0)
        def _():
            x_copy(mine, z, c, h, down_sem, down).start()

        x_copy(mine, z, c, h, side_sem, sibling).start()

    def each_chunk(body):
        def step(j, carry):
            body(j)
            return carry

        lax.fori_loop(0, CHUNKS, step, 0)

    each_chunk(lambda j: g_copy(sibling, j).start())

    def send_g_near(chip):
        def one(j):
            for core in range(2):
                g_copy(chip * 2 + core, j).start()

        each_chunk(one)

    def is_end(chip):
        return (chip == 0) | (chip == nz - 1)

    def is_far(chip):
        return (chip >= 0) & (chip < nz) & ((chip > z + 1) | (chip < z - 1))

    def send_g_middle(j):
        def one(chip, carry):
            @pl.when(is_far(chip))
            def _():
                for core in range(2):
                    g_copy(chip * 2 + core, j).start()

            return carry

        lax.fori_loop(1, nz - 1, one, 0)

    def send_g_end(level, first, last):
        for chip in (0, nz - 1):

            @pl.when(is_far(chip))
            def _():
                pl.semaphore_wait(ready.at[level, chip], 2)

                def one(j, carry):
                    for core in range(2):
                        g_copy(chip * 2 + core, j).start()
                    return carry

                lax.fori_loop(first, last, one, 0)

    def tell_far(level):
        def one(chip, carry):
            @pl.when(is_far(chip))
            def _():
                for core in range(2):
                    pl.semaphore_signal(
                        ready.at[level, z],
                        inc=1,
                        device_id={"fsdp": chip * 2 + core},
                        device_id_type=MESH,
                    )

            return carry

        @pl.when(is_end(z))
        def _():
            lax.fori_loop(0, nz, one, 0)

    et = min(512, depth)

    def make_weff(j):
        sw_load(j).wait()
        dw_load(j).wait()

        def one(i, carry):
            at = pl.ds(pl.multiple_of(i * et, et), et)
            weff[at, cols(j)] = (
                swb[lax.rem(j, 2), at, :].astype(F32) * tb[j, at, :].astype(F32)
            ).astype(BF16)
            return carry

        lax.fori_loop(0, depth // et, one, 0)

        @pl.when(j + 2 < CHUNKS)
        def _():
            sw_load(j + 2).start()

    each_chunk(make_weff)
    for j in range(2):
        sw_load(j).start()
    own_x.wait()
    own_g.wait()

    count = count_ref[0]
    scale = lax.rsqrt(jnp.full((1, 1), count, jnp.int32).astype(F32))

    def wait_x_half(chip, core, h):
        slot = x_slot(chip, core, h)
        x_copy(slot, chip, core, h, side_sem, sibling).wait_recv()

    def wait_x(chip, core):
        for h in range(HALVES):
            wait_x_half(chip, core, h)

    def wait_g(chip, core, j):
        pltpu.make_async_remote_copy(
            src_ref=gs.at[core_rows(chip, core), cols(j)],
            dst_ref=gs.at[core_rows(chip, core), cols(j)],
            send_sem=gsend_sem.at[me, j],
            recv_sem=g_sem.at[chip * 2 + core, j],
            device_id={"fsdp": sibling},
            device_id_type=MESH,
        ).wait_recv()

    def pre(chip, j):
        wait_g(chip, 1 - c, j)

        @pl.when(chip != z)
        def _():
            wait_g(chip, c, j)

        here = chip_rows(chip)
        preact = jnp.dot(xs[here, :], weff[:, cols(j)], preferred_element_type=F32)
        sigma = jax.nn.sigmoid(preact)
        position = chip * (2 * rows) + lax.broadcasted_iota(jnp.int32, preact.shape, 0)
        slope = gs[here, cols(j)].astype(F32) * sigma * (1.0 + preact * (1.0 - sigma))
        gs[here, cols(j)] = jnp.where(position < count, slope, 0.0).astype(BF16)

    def sib_copy(chip, slot, pc):
        return pltpu.make_async_remote_copy(
            src_ref=dxb.at[slot, pc, pl.ds(pl.multiple_of((1 - c) * rows, rows), rows)],
            dst_ref=sib.at[chip, pc],
            send_sem=sib_send.at[chip, pc],
            recv_sem=sib_recv.at[chip, pc],
            device_id={"fsdp": sibling},
            device_id_type=MESH,
        )

    def chain_copy(slot, chip, pc, target):
        return pltpu.make_async_remote_copy(
            src_ref=sib.at[chip, pc],
            dst_ref=chain.at[slot, pc],
            send_sem=ch_send.at[chip, pc],
            recv_sem=ch_recv.at[slot, pc],
            device_id={"fsdp": target},
            device_id_type=MESH,
        )

    def send_up(chip, pc):
        return chain_copy(chip, chip, pc, lax.rem(me + 2, n))

    def send_down(chip, pc):
        return chain_copy(jnp.where(chip == z - 1, nz, chip), chip, pc, lax.rem(me + n - 2, n))

    def pair_sum(chip, slot, pc):
        sib_copy(chip, slot, pc).wait_send()
        sib_copy(chip, slot, pc).wait_recv()
        own = dxb[slot, pc, pl.ds(pl.multiple_of(c * rows, rows), rows), :]
        sib[chip, pc] = (own.astype(F32) + sib[chip, pc].astype(F32)).astype(BF16)

        @pl.when((z == 0) & (chip > z))
        def _():
            send_up(chip, pc).start()

        @pl.when((z == nz - 1) & (chip < z))
        def _():
            send_down(chip, pc).start()

    def each_piece(body):
        def step(pc, carry):
            body(pc)
            return carry

        lax.fori_loop(0, PIECES, step, 0)

    def back(chip, turn, before, pending):
        slot = lax.rem(turn, 2)

        def one(group, carry):
            wide = PAIR * pw
            at = pl.ds(pl.multiple_of(group * wide, wide), wide)
            partial = lax.dot_general(
                gs[chip_rows(chip), :],
                weff[at, :],
                (((1,), (1,)), ((), ())),
                preferred_element_type=F32,
            ).astype(BF16)
            for i in range(PAIR):
                pc = group * PAIR + i
                dxb[slot, pc] = partial[:, i * pw : (i + 1) * pw]
                sib_copy(chip, slot, pc).start()

            @pl.when(pending)
            def _():
                for i in range(PAIR):
                    pair_sum(before, 1 - slot, group * PAIR + i)

            return carry

        lax.fori_loop(0, PIECES // PAIR, one, 0)

    wait_x(z, 1 - c)
    each_chunk(lambda j: pre(z, j))
    back(z, 0, z, False)

    def receive(chip, h, forward, target, sem):
        wait_x_half(chip, c, h)
        slot = x_slot(chip, c, h)

        @pl.when(forward)
        def _():
            x_copy(slot, chip, c, h, sem, target).start()

        x_copy(slot, chip, c, h, side_sem, sibling).start()

    def receive_both(distance, h):
        below, above = z - distance, z + distance

        @pl.when(below >= 0)
        def _():
            receive(below, h, z + 1 < nz, up, up_sem)

        @pl.when(above < nz)
        def _():
            receive(above, h, z > 0, down, down_sem)

    @pl.when(z == 0)
    def _():
        send_g_near(z + 1)

    @pl.when(z == nz - 1)
    def _():
        send_g_near(z - 1)

    def gather_step(distance, carry):
        for h in range(HALVES):
            receive_both(distance, h)

        @pl.when((distance == 1) & (z > 0) & (z < nz - 1))
        def _():
            send_g_near(z + 1)
            send_g_near(z - 1)

        @pl.when(distance == nz - 2)
        def _():
            each_chunk(send_g_middle)

        return carry

    lax.fori_loop(1, nz - 1, gather_step, 0)

    def near(side, carry):
        turn, before = carry
        chip = z - 1 + 2 * side
        valid = (chip >= 0) & (chip < nz)

        @pl.when(valid)
        def _():
            wait_x(chip, 1 - c)
            each_chunk(lambda j: pre(chip, j))
            back(chip, turn, before, True)

        return jnp.where(valid, turn + 1, turn), jnp.where(valid, chip, before)

    turns, last = lax.fori_loop(0, 2, near, (1, z))

    for h in range(HALVES):
        receive_both(nz - 1, h)
        if h == 0:
            tell_far(0)
            send_g_end(0, 0, 1)
    tell_far(1)

    @pl.when(is_end(z))
    def _():
        send_g_end(1, 1, CHUNKS)

    def far_chip(k):
        chip = jnp.where(z < nz // 2, nz - 1 - k, k)
        return chip, is_far(chip)

    order = sorted(range(nd), key=lambda m: (-bin(m).count("1"), m))

    def bit_order(p):
        return [(p + s) % bits for s in range(bits)]

    def sent_at(m, p):
        return next((s for s, b in enumerate(bit_order(p)) if m >> b & 1), bits)

    index = [{} for _ in range(parts)]
    for p in range(parts):
        for m in range(1, nd):
            s = sent_at(m, p)
            index[p][s, m ^ (1 << bit_order(p)[s])] = len(index[p])

    def tile_rows(m, q):
        return pl.ds(pl.multiple_of(flip(dom, m) * block + q * tile, tile), tile)

    def block_rows(m):
        return pl.ds(pl.multiple_of(flip(dom, m) * block, block), block)

    def d_copy(j, m, q):
        p = q % parts
        s = sent_at(m, p)
        bit = 1 << bit_order(p)[s]
        at = index[p][s, m ^ bit]
        return pltpu.make_async_remote_copy(
            src_ref=tb.at[j, tile_rows(m, q)],
            dst_ref=rb.at[at, j, pl.ds(q * tile, tile)],
            send_sem=d_send.at[at, j, q],
            recv_sem=d_recv.at[at, j, q],
            device_id={"dom": flip(dom, bit)},
            device_id_type=MESH,
        )

    def arrived(j, m, q, steps):
        p = q % parts
        total = tb[j, tile_rows(m, q), :].astype(F32)
        for s in range(steps):
            at = index[p][s, m]
            here = pl.ds(q * tile, tile)
            pltpu.make_async_remote_copy(
                src_ref=rb.at[at, j, here],
                dst_ref=rb.at[at, j, here],
                send_sem=d_send.at[at, j, q],
                recv_sem=d_recv.at[at, j, q],
                device_id={"dom": flip(dom, 1 << bit_order(p)[s])},
                device_id_type=MESH,
            ).wait_recv()
            total = total + rb[at, j, here, :].astype(F32)
        return total

    def dom_store(j, m):
        return pltpu.make_async_copy(
            swb.at[lax.rem(j, 2), block_rows(m)],
            dom_out.at[block_rows(m), cols(j)],
            dom_sem.at[j, m],
        )

    def weight_chunk(j):
        sw_load(j).wait()

        @pl.when((j >= 1) & (j + 1 < CHUNKS))
        def _():
            for m in range(nd):
                dom_store(j - 1, m).wait()
            sw_load(j + 1).start()

        slot = lax.rem(j, 2)
        for m in order:
            at = block_rows(m)
            scaled = scale * lax.dot_general(
                xs[:, at], gs[:, cols(j)], (((0,), (0,)), ((), ())), preferred_element_type=F32
            )
            tb[j, at, :] = (scaled * tb[j, at, :].astype(F32)).astype(BF16)
            for q in range(pieces):
                if sent_at(m, q % parts) == 0:
                    d_copy(j, m, q).start()
            swb[slot, at, :] = (scaled * swb[slot, at, :].astype(F32)).astype(BF16)
            dom_store(j, m).start()

    def wait_far_x(k, carry):
        chip, valid = far_chip(k)

        @pl.when(valid)
        def _():
            wait_x(chip, 1 - c)

        return carry

    lax.fori_loop(0, nz, wait_far_x, 0)

    def chunk_step(j):
        @pl.when((j == CHUNKS // 2) & (z > 0) & (z < nz - 1))
        def _():
            send_g_end(1, 1, CHUNKS)

        def far_pre(k, carry):
            chip, valid = far_chip(k)

            @pl.when(valid)
            def _():
                pre(chip, j)

            return carry

        lax.fori_loop(0, nz, far_pre, 0)

        @pl.when(j == 0)
        def _():
            each_piece(lambda pc: pair_sum(last, lax.rem(turns - 1, 2), pc))

        @pl.when(j == CHUNKS - 1)
        def _():
            def far_back(k, carry):
                turn, before, pending = carry
                chip, valid = far_chip(k)

                @pl.when(valid)
                def _():
                    back(chip, turn, before, pending > 0)

                return (
                    jnp.where(valid, turn + 1, turn),
                    jnp.where(valid, chip, before),
                    jnp.where(valid, 1, pending),
                )

            turn, before, pending = lax.fori_loop(0, nz, far_back, (turns, last, 0))

            @pl.when(pending > 0)
            def _():
                each_piece(lambda pc: pair_sum(before, lax.rem(turn - 1, 2), pc))

        weight_chunk(j)

    each_chunk(chunk_step)

    hops = (nz - 1) * PIECES

    def take(slot, chip, pc):
        pltpu.make_async_remote_copy(
            src_ref=chain.at[slot, pc],
            dst_ref=chain.at[slot, pc],
            send_sem=ch_send.at[chip, pc],
            recv_sem=ch_recv.at[slot, pc],
            device_id={"fsdp": sibling},
            device_id_type=MESH,
        ).wait_recv()
        sib[chip, pc] = (sib[chip, pc].astype(F32) + chain[slot, pc].astype(F32)).astype(BF16)

    def turn_of(step):
        rising = jnp.where(step < PIECES, 1, nz - lax.div(step, PIECES))
        return rising, lax.rem(step, PIECES), (step >= 0) & (step < hops)

    def hop(t):
        rising, pc, valid = turn_of(t - (z - 1))

        @pl.when(valid & (z > 0) & (rising >= z))
        def _():
            take(rising, rising, pc)

            @pl.when(rising > z)
            def _():
                send_up(rising, pc).start()

        mirrored, pd, due = turn_of(t - (nz - 2 - z))
        falling = nz - 1 - mirrored

        @pl.when(due & (z < nz - 1) & (falling <= z))
        def _():
            take(jnp.where(falling == z, nz, falling), falling, pd)

            @pl.when(falling < z)
            def _():
                send_down(falling, pd).start()

    def relay(j):
        for s in range(1, bits):
            for m in order:
                for q in range(pieces):
                    if m and sent_at(m, q % parts) == s:
                        total = arrived(j, m, q, s).astype(BF16)
                        tb[j, tile_rows(m, q), :] = total
                        d_copy(j, m, q).start()

    def shared_store(j):
        return pltpu.make_async_copy(shv.at[j], shared_out.at[:, cols(j)], out_sem.at[j])

    spread = PIECES // 2

    def tail_step(t, carry):
        hop(t)
        mark = t - (PIECES - 1)

        @pl.when((mark >= 0) & (lax.rem(mark, spread) == 0) & (mark < spread * CHUNKS))
        def _():
            relay(lax.div(mark, spread))

        return carry

    lax.fori_loop(0, max(hops + nz - 2, PIECES - 1 + spread * CHUNKS), tail_step, 0)

    def in_store(pc):
        return pltpu.make_async_copy(sib.at[z, pc], in_out.at[:, depth_cols(pc)], in_sem.at[pc])

    each_piece(lambda pc: in_store(pc).start())

    def final(j):
        for q in range(pieces):
            shv[j, pl.ds(q * tile, tile), :] = arrived(j, 0, q, bits)
        shared_store(j).start()

    each_chunk(final)

    for j in range(max(0, CHUNKS - 2), CHUNKS):
        for m in range(nd):
            dom_store(j, m).wait()

    def drain_chip(chip, carry):
        for h in range(HALVES):
            slot = x_slot(chip, c, h)

            @pl.when((chip <= z) & (z + 1 < nz))
            def _():
                x_copy(slot, chip, c, h, up_sem, up).wait_send()

            @pl.when((chip >= z) & (z > 0))
            def _():
                x_copy(slot, chip, c, h, down_sem, down).wait_send()

            x_copy(slot, chip, c, h, side_sem, sibling).wait_send()

        def sums(pc):
            @pl.when(chip > z)
            def _():
                send_up(chip, pc).wait_send()

            @pl.when(chip < z)
            def _():
                send_down(chip, pc).wait_send()

        each_piece(sums)
        return carry

    lax.fori_loop(0, nz, drain_chip, 0)

    def drain_g(k, carry):
        each_chunk(lambda j: g_copy(lax.rem(me + k, n), j).wait_send())
        return carry

    lax.fori_loop(1, n, drain_g, 0)

    def drain_d(j):
        for m in range(1, nd):
            for q in range(pieces):
                d_copy(j, m, q).wait_send()
        shared_store(j).wait()

    each_chunk(drain_d)
    each_piece(lambda pc: in_store(pc).wait())


def fused(n, nd, x, g, sw, dw, count):
    rows, depth = x.shape
    width = sw.shape[1]
    nz = n // 2
    total = n * rows
    block = depth // nd
    bits = nd.bit_length() - 1
    tile = min(TILE, block // min(2, bits))
    pieces = block // tile
    cw, pw = width // CHUNKS, depth // PIECES
    any_spec = pl.BlockSpec(memory_space=pl.ANY)
    dma = pltpu.SemaphoreType.DMA
    vmem = pltpu.VMEM
    return pl.pallas_call(
        functools.partial(fused_kernel, n, nd),
        out_shape=(
            jax.ShapeDtypeStruct((block, width), F32),
            jax.ShapeDtypeStruct((depth, width), BF16),
            jax.ShapeDtypeStruct((rows, depth), BF16),
        ),
        in_specs=[any_spec] * 4 + [pl.BlockSpec(memory_space=pltpu.SMEM)],
        out_specs=(any_spec,) * 3,
        scratch_shapes=[
            vmem((total, depth), BF16),
            vmem((total, width), BF16),
            vmem((depth, width), BF16),
            vmem((CHUNKS, depth, cw), BF16),
            vmem((nd - 1, CHUNKS, block, cw), BF16),
            vmem((nz, PIECES, rows, pw), BF16),
            vmem((nz + 1, PIECES, rows, pw), BF16),
            vmem((2, PIECES, 2 * rows, pw), BF16),
            vmem((2, depth, cw), BF16),
            vmem((CHUNKS, block, cw), F32),
            dma((nz, HALVES)),
            dma((nz, HALVES)),
            dma((nz, HALVES)),
            dma((n, HALVES)),
            dma((n, CHUNKS)),
            dma((n, CHUNKS)),
            dma((2,)),
            dma((CHUNKS,)),
            dma((CHUNKS,)),
            dma((nz, PIECES)),
            dma((nz, PIECES)),
            dma((nz, PIECES)),
            dma((nz + 1, PIECES)),
            dma((nd - 1, CHUNKS, pieces)),
            dma((nd - 1, CHUNKS, pieces)),
            dma((CHUNKS, nd)),
            dma((CHUNKS,)),
            dma((PIECES,)),
            pltpu.SemaphoreType.REGULAR((2, nz)),
        ],
        compiler_params=pltpu.CompilerParams(
            collective_id=0, has_side_effects=True, vmem_limit_bytes=63 * 1024 * 1024
        ),
        name="gather_backprop_reduce",
    )(x, g, sw, dw, count)


def store_kernel(a_ref, b_ref, c_ref, a_out, b_out, c_out):
    a_out[...] = a_ref[...]
    b_out[...] = b_ref[...]
    c_out[...] = c_ref[...]


def store_results(*arrays):
    steps = 8
    specs = tuple(
        pl.BlockSpec((a.shape[0] // steps, a.shape[1]), lambda i: (i, 0)) for a in arrays
    )
    return pl.pallas_call(
        store_kernel,
        grid=(steps,),
        out_shape=tuple(jax.ShapeDtypeStruct(a.shape, a.dtype) for a in arrays),
        in_specs=specs,
        out_specs=specs,
        compiler_params=pltpu.CompilerParams(vmem_limit_bytes=63 * 1024 * 1024),
        name="store_results",
    )(*arrays)


def solution(mesh):
    n, nd = mesh.shape["fsdp"], mesh.shape["dom"]

    def body(inputs, cotangent, shared_weight, domain_weight, row_counts):
        results = fused(
            n, nd, inputs[0], cotangent[0], shared_weight, domain_weight[0], row_counts
        )
        shared_grad, domain_grad, input_grad = store_results(*results)
        return (shared_grad, domain_grad[None], input_grad[None])

    return jax.shard_map(
        body,
        mesh=mesh,
        in_specs=(
            P("dom", "fsdp", None),
            P("dom", "fsdp", None),
            P(None, "fsdp"),
            P("dom", None, "fsdp"),
            P("dom"),
        ),
        out_specs=(P("dom", "fsdp"), P("dom", None, "fsdp"), P("dom", "fsdp", None)),
        check_vma=False,
    )
```

```python
import functools

import jax
import jax.numpy as jnp
from jax import lax
from jax.experimental import pallas as pl
from jax.experimental.pallas import tpu as pltpu
from jax.sharding import PartitionSpec as P

MESH = pl.DeviceIdType.MESH
F32 = jnp.float32
BF16 = jnp.bfloat16
CHUNKS = 4
PIECES = 8
PAIR = 2
HALVES = 2
EARLY = 2
STORES = 8
TILE = 256


def fused_kernel(
    n, nd, x_ref, g_ref, sw_ref, dw_ref, count_ref, shared_out, dom_out, in_out,
    xs, gs, weff, tb, rb, sib, chain, dxb, swb, shv,
    up_sem, down_sem, side_sem, x_sem, gsend_sem, g_sem, own_sem, sw_sem, dw_sem,
    sib_send, sib_recv, ch_send, ch_recv, d_send, d_recv, dom_sem, out_sem, in_sem, ready,
):
    me, dom = lax.axis_index("fsdp"), lax.axis_index("dom")
    nz = n // 2
    z, c = lax.div(me, 2), lax.rem(me, 2)
    up, down, sibling = me + 2, me - 2, z * 2 + (1 - c)
    rows, depth = x_ref.shape
    width = sw_ref.shape[1]
    cw = width // CHUNKS
    pw = depth // PIECES
    block = depth // nd
    bits = nd.bit_length() - 1
    parts = min(2, bits)
    tile = min(TILE, block // parts)
    pieces = block // tile

    def flip(value, mask):
        for b in range(bits):
            if mask >> b & 1:
                value = value + (1 << b) - (2 << b) * lax.rem(lax.div(value, 1 << b), 2)
        return value

    barrier = pltpu.get_barrier_semaphore()

    def greet(k, carry):
        pl.semaphore_signal(
            barrier, inc=1, device_id={"fsdp": lax.rem(me + k, n)}, device_id_type=MESH
        )
        return carry

    lax.fori_loop(1, n, greet, 0)
    for b in range(bits):
        pl.semaphore_signal(
            barrier, inc=1, device_id={"dom": flip(dom, 1 << b)}, device_id_type=MESH
        )

    def cols(j):
        return pl.ds(pl.multiple_of(j * cw, cw), cw)

    def depth_cols(pc):
        return pl.ds(pl.multiple_of(pc * pw, pw), pw)

    def chip_rows(chip):
        return pl.ds(pl.multiple_of(chip * (2 * rows), 2 * rows), 2 * rows)

    def core_rows(chip, core):
        return pl.ds(pl.multiple_of((chip * 2 + core) * rows, rows), rows)

    def sw_load(j):
        return pltpu.make_async_copy(sw_ref.at[:, cols(j)], swb.at[lax.rem(j, 2)], sw_sem.at[j])

    def dw_load(j):
        return pltpu.make_async_copy(dw_ref.at[:, cols(j)], tb.at[j], dw_sem.at[j])

    own_x = pltpu.make_async_copy(x_ref, xs.at[core_rows(z, c)], own_sem.at[0])
    own_g = pltpu.make_async_copy(
        g_ref.at[:, pl.ds(pl.multiple_of(me * width, width), width)],
        gs.at[core_rows(z, c)],
        own_sem.at[1],
    )
    for j in range(CHUNKS):
        if j < 2:
            sw_load(j).start()
        dw_load(j).start()
    own_x.start()
    own_g.start()

    pl.semaphore_wait(barrier, n - 1 + bits)

    part = rows // HALVES

    def x_slot(chip, core, h):
        at = (chip * 2 + core) * rows + h * part
        return xs.at[pl.ds(pl.multiple_of(at, part), part)]

    def x_copy(src, chip, core, h, sem, target):
        return pltpu.make_async_remote_copy(
            src_ref=src,
            dst_ref=x_slot(chip, core, h),
            send_sem=sem.at[chip, h],
            recv_sem=x_sem.at[chip * 2 + core, h],
            device_id={"fsdp": target},
            device_id_type=MESH,
        )

    def g_copy(target, j):
        at = pl.ds(pl.multiple_of(target * width + j * cw, cw), cw)
        return pltpu.make_async_remote_copy(
            src_ref=g_ref.at[:, at],
            dst_ref=gs.at[core_rows(z, c), cols(j)],
            send_sem=gsend_sem.at[target, j],
            recv_sem=g_sem.at[me, j],
            device_id={"fsdp": target},
            device_id_type=MESH,
        )

    for h in range(HALVES):
        mine = x_ref.at[pl.ds(h * part, part)]

        @pl.when(z + 1 < nz)
        def _():
            x_copy(mine, z, c, h, up_sem, up).start()

        @pl.when(z > 0)
        def _():
            x_copy(mine, z, c, h, down_sem, down).start()

        x_copy(mine, z, c, h, side_sem, sibling).start()

    def each_chunk(body):
        def step(j, carry):
            body(j)
            return carry

        lax.fori_loop(0, CHUNKS, step, 0)

    each_chunk(lambda j: g_copy(sibling, j).start())

    def send_g_near(chip):
        def one(j):
            for core in range(2):
                g_copy(chip * 2 + core, j).start()

        each_chunk(one)

    def is_end(chip):
        return (chip == 0) | (chip == nz - 1)

    def is_far(chip):
        return (chip >= 0) & (chip < nz) & ((chip > z + 1) | (chip < z - 1))

    def send_g_middle(j):
        def one(chip, carry):
            @pl.when(is_far(chip))
            def _():
                for core in range(2):
                    g_copy(chip * 2 + core, j).start()

            return carry

        lax.fori_loop(1, nz - 1, one, 0)

    def send_g_end(level):
        for chip in (0, nz - 1):
            across = is_end(z)
            mine = jnp.logical_not(across) if level == 2 else True

            @pl.when(is_far(chip) & mine)
            def _():
                pl.semaphore_wait(ready.at[level, chip], 2)

                def one(j, carry):
                    for core in range(2):
                        g_copy(chip * 2 + core, j).start()
                    return carry

                until = (1, jnp.where(across, CHUNKS, 2), CHUNKS)[level]
                lax.fori_loop(level, until, one, 0)

    def tell_far(level):
        def one(chip, carry):
            theirs = jnp.logical_not(is_end(chip)) if level == 2 else True

            @pl.when(is_far(chip) & theirs)
            def _():
                for core in range(2):
                    pl.semaphore_signal(
                        ready.at[level, z],
                        inc=1,
                        device_id={"fsdp": chip * 2 + core},
                        device_id_type=MESH,
                    )

            return carry

        @pl.when(is_end(z))
        def _():
            lax.fori_loop(0, nz, one, 0)

    et = min(512, depth)

    def make_weff(j):
        sw_load(j).wait()
        dw_load(j).wait()

        def one(i, carry):
            at = pl.ds(pl.multiple_of(i * et, et), et)
            weff[at, cols(j)] = (
                swb[lax.rem(j, 2), at, :].astype(F32) * tb[j, at, :].astype(F32)
            ).astype(BF16)
            return carry

        lax.fori_loop(0, depth // et, one, 0)

        @pl.when(j + 2 < CHUNKS)
        def _():
            sw_load(j + 2).start()

    each_chunk(make_weff)
    for j in range(2):
        sw_load(j).start()
    own_x.wait()
    own_g.wait()

    count = count_ref[0]
    scale = lax.rsqrt(jnp.full((1, 1), count, jnp.int32).astype(F32))

    def wait_x_half(chip, core, h):
        slot = x_slot(chip, core, h)
        x_copy(slot, chip, core, h, side_sem, sibling).wait_recv()

    def wait_x(chip, core):
        for h in range(HALVES):
            wait_x_half(chip, core, h)

    def wait_g(chip, core, j):
        pltpu.make_async_remote_copy(
            src_ref=gs.at[core_rows(chip, core), cols(j)],
            dst_ref=gs.at[core_rows(chip, core), cols(j)],
            send_sem=gsend_sem.at[me, j],
            recv_sem=g_sem.at[chip * 2 + core, j],
            device_id={"fsdp": sibling},
            device_id_type=MESH,
        ).wait_recv()

    def pre(chip, j):
        wait_g(chip, 1 - c, j)

        @pl.when(chip != z)
        def _():
            wait_g(chip, c, j)

        here = chip_rows(chip)
        preact = jnp.dot(xs[here, :], weff[:, cols(j)], preferred_element_type=F32)
        sigma = jax.nn.sigmoid(preact)
        position = chip * (2 * rows) + lax.broadcasted_iota(jnp.int32, preact.shape, 0)
        slope = gs[here, cols(j)].astype(F32) * sigma * (1.0 + preact * (1.0 - sigma))
        gs[here, cols(j)] = jnp.where(position < count, slope, 0.0).astype(BF16)

    def sib_copy(chip, slot, pc):
        return pltpu.make_async_remote_copy(
            src_ref=dxb.at[slot, pc, pl.ds(pl.multiple_of((1 - c) * rows, rows), rows)],
            dst_ref=sib.at[chip, pc],
            send_sem=sib_send.at[chip, pc],
            recv_sem=sib_recv.at[chip, pc],
            device_id={"fsdp": sibling},
            device_id_type=MESH,
        )

    def chain_copy(slot, chip, pc, target):
        return pltpu.make_async_remote_copy(
            src_ref=sib.at[chip, pc],
            dst_ref=chain.at[slot, pc],
            send_sem=ch_send.at[chip, pc],
            recv_sem=ch_recv.at[slot, pc],
            device_id={"fsdp": target},
            device_id_type=MESH,
        )

    def send_up(chip, pc):
        return chain_copy(chip, chip, pc, lax.rem(me + 2, n))

    def send_down(chip, pc):
        return chain_copy(jnp.where(chip == z - 1, nz, chip), chip, pc, lax.rem(me + n - 2, n))

    def pair_sum(chip, slot, pc):
        sib_copy(chip, slot, pc).wait_send()
        sib_copy(chip, slot, pc).wait_recv()
        own = dxb[slot, pc, pl.ds(pl.multiple_of(c * rows, rows), rows), :]
        sib[chip, pc] = (own.astype(F32) + sib[chip, pc].astype(F32)).astype(BF16)

        @pl.when((z == 0) & (chip > z))
        def _():
            send_up(chip, pc).start()

        @pl.when((z == nz - 1) & (chip < z))
        def _():
            send_down(chip, pc).start()

    def each_piece(body):
        def step(pc, carry):
            body(pc)
            return carry

        lax.fori_loop(0, PIECES, step, 0)

    def back(chip, turn, before, pending):
        slot = lax.rem(turn, 2)

        def one(group, carry):
            wide = PAIR * pw
            at = pl.ds(pl.multiple_of(group * wide, wide), wide)
            partial = lax.dot_general(
                gs[chip_rows(chip), :],
                weff[at, :],
                (((1,), (1,)), ((), ())),
                preferred_element_type=F32,
            ).astype(BF16)
            for i in range(PAIR):
                pc = group * PAIR + i
                dxb[slot, pc] = partial[:, i * pw : (i + 1) * pw]
                sib_copy(chip, slot, pc).start()

            @pl.when(pending)
            def _():
                for i in range(PAIR):
                    pair_sum(before, 1 - slot, group * PAIR + i)

            return carry

        lax.fori_loop(0, PIECES // PAIR, one, 0)

    wait_x(z, 1 - c)
    each_chunk(lambda j: pre(z, j))
    back(z, 0, z, False)

    def receive(chip, h, forward, target, sem):
        wait_x_half(chip, c, h)
        slot = x_slot(chip, c, h)

        @pl.when(forward)
        def _():
            x_copy(slot, chip, c, h, sem, target).start()

        x_copy(slot, chip, c, h, side_sem, sibling).start()

    def receive_both(distance, h):
        below, above = z - distance, z + distance

        @pl.when(below >= 0)
        def _():
            receive(below, h, z + 1 < nz, up, up_sem)

        @pl.when(above < nz)
        def _():
            receive(above, h, z > 0, down, down_sem)

    @pl.when(z == 0)
    def _():
        send_g_near(z + 1)

    @pl.when(z == nz - 1)
    def _():
        send_g_near(z - 1)

    def gather_step(distance, carry):
        for h in range(HALVES):
            receive_both(distance, h)

        @pl.when((distance == 1) & (z > 0) & (z < nz - 1))
        def _():
            send_g_near(z + 1)
            send_g_near(z - 1)

        @pl.when(distance == nz - 2)
        def _():
            each_chunk(send_g_middle)

        return carry

    lax.fori_loop(1, nz - 1, gather_step, 0)

    def near(side, carry):
        turn, before = carry
        chip = z - 1 + 2 * side
        valid = (chip >= 0) & (chip < nz)

        @pl.when(valid)
        def _():
            wait_x(chip, 1 - c)
            each_chunk(lambda j: pre(chip, j))
            back(chip, turn, before, True)

        return jnp.where(valid, turn + 1, turn), jnp.where(valid, chip, before)

    turns, last = lax.fori_loop(0, 2, near, (1, z))

    def flush(chip, turn, first, last):
        def one(pc, carry):
            pair_sum(chip, lax.rem(turn, 2), pc)
            return carry

        lax.fori_loop(first, last, one, 0)

    flush(last, turns - 1, 0, PIECES // 4)
    for h in range(HALVES):
        receive_both(nz - 1, h)
        if h == 0:
            tell_far(0)
            send_g_end(0)
            flush(last, turns - 1, PIECES // 4, PIECES)
    tell_far(1)

    @pl.when(is_end(z))
    def _():
        send_g_end(1)

    farthest = jnp.where(z < nz // 2, nz - 1, 0)

    def each_far(body):
        def one(k, carry):
            chip = jnp.where(z < nz // 2, nz - 1 - k, k)
            return body(chip, is_far(chip), carry)

        return lambda carry: lax.fori_loop(0, nz, one, carry)

    order = sorted(range(nd), key=lambda m: (-bin(m).count("1"), m))

    def bit_order(p):
        return [(p + s) % bits for s in range(bits)]

    def sent_at(m, p):
        return next((s for s, b in enumerate(bit_order(p)) if m >> b & 1), bits)

    index = [{} for _ in range(parts)]
    for p in range(parts):
        for m in range(1, nd):
            s = sent_at(m, p)
            index[p][s, m ^ (1 << bit_order(p)[s])] = len(index[p])

    def tile_rows(m, q):
        return pl.ds(pl.multiple_of(flip(dom, m) * block + q * tile, tile), tile)

    def block_rows(m):
        return pl.ds(pl.multiple_of(flip(dom, m) * block, block), block)

    def d_copy(j, m, q):
        p = q % parts
        s = sent_at(m, p)
        bit = 1 << bit_order(p)[s]
        at = index[p][s, m ^ bit]
        return pltpu.make_async_remote_copy(
            src_ref=tb.at[j, tile_rows(m, q)],
            dst_ref=rb.at[at, j, pl.ds(q * tile, tile)],
            send_sem=d_send.at[at, j, q],
            recv_sem=d_recv.at[at, j, q],
            device_id={"dom": flip(dom, bit)},
            device_id_type=MESH,
        )

    def arrived(j, m, q, steps):
        p = q % parts
        total = tb[j, tile_rows(m, q), :].astype(F32)
        for s in range(steps):
            at = index[p][s, m]
            here = pl.ds(q * tile, tile)
            pltpu.make_async_remote_copy(
                src_ref=rb.at[at, j, here],
                dst_ref=rb.at[at, j, here],
                send_sem=d_send.at[at, j, q],
                recv_sem=d_recv.at[at, j, q],
                device_id={"dom": flip(dom, 1 << bit_order(p)[s])},
                device_id_type=MESH,
            ).wait_recv()
            total = total + rb[at, j, here, :].astype(F32)
        return total

    def dom_store(j, m):
        return pltpu.make_async_copy(
            swb.at[lax.rem(j, 2), block_rows(m)],
            dom_out.at[block_rows(m), cols(j)],
            dom_sem.at[j, m],
        )

    def weight_chunk(j):
        sw_load(j).wait()

        @pl.when((j >= 1) & (j + 1 < CHUNKS))
        def _():
            for m in range(nd):
                dom_store(j - 1, m).wait()
            sw_load(j + 1).start()

        slot = lax.rem(j, 2)
        for m in order:
            at = block_rows(m)
            scaled = scale * lax.dot_general(
                xs[:, at], gs[:, cols(j)], (((0,), (0,)), ((), ())), preferred_element_type=F32
            )
            tb[j, at, :] = (scaled * tb[j, at, :].astype(F32)).astype(BF16)
            for q in range(pieces):
                if sent_at(m, q % parts) == 0:
                    d_copy(j, m, q).start()
            swb[slot, at, :] = (scaled * swb[slot, at, :].astype(F32)).astype(BF16)
            dom_store(j, m).start()

    def wait_far_x(chip, valid, carry):
        @pl.when(valid)
        def _():
            wait_x(chip, 1 - c)

        return carry

    each_far(wait_far_x)(0)

    def chunk_step(j):
        @pl.when((j == 1) & (z > 0) & (z < nz - 1))
        def _():
            send_g_end(1)

        @pl.when((j == 2) & (z > 0) & (z < nz - 1))
        def _():
            send_g_end(2)

        @pl.when(j <= EARLY)
        def _():
            def some(i, carry):
                pre(farthest, i)
                return carry

            lax.fori_loop(j, jnp.where(j == EARLY, CHUNKS, j + 1), some, 0)

        @pl.when(j == 0)
        def _():
            tell_far(2)

        @pl.when(j == EARLY)
        def _():
            back(farthest, turns, farthest, False)

        def far_pre(chip, valid, carry):
            @pl.when(valid & (chip != farthest))
            def _():
                pre(chip, j)

            return carry

        each_far(far_pre)(0)

        @pl.when(j == EARLY)
        def _():
            flush(farthest, turns, 0, PIECES)

        @pl.when(j == CHUNKS - 1)
        def _():
            def far_back(chip, valid, carry):
                turn, before, pending = carry
                new = valid & (chip != farthest)

                @pl.when(new)
                def _():
                    back(chip, turn, before, pending > 0)

                return (
                    jnp.where(new, turn + 1, turn),
                    jnp.where(new, chip, before),
                    jnp.where(new, 1, pending),
                )

            turn, before, pending = each_far(far_back)((turns + 1, farthest, 0))

            @pl.when(pending > 0)
            def _():
                flush(before, turn - 1, 0, PIECES)

        weight_chunk(j)

    each_chunk(chunk_step)

    hops = (nz - 1) * PIECES

    def take(slot, chip, pc):
        pltpu.make_async_remote_copy(
            src_ref=chain.at[slot, pc],
            dst_ref=chain.at[slot, pc],
            send_sem=ch_send.at[chip, pc],
            recv_sem=ch_recv.at[slot, pc],
            device_id={"fsdp": sibling},
            device_id_type=MESH,
        ).wait_recv()
        sib[chip, pc] = (sib[chip, pc].astype(F32) + chain[slot, pc].astype(F32)).astype(BF16)

    def turn_of(step):
        turn = lax.div(step, PIECES)
        rising = jnp.where(turn == 0, 1, nz - turn)
        return rising, lax.rem(step, PIECES), (step >= 0) & (step < hops)

    def hop(t):
        rising, pc, valid = turn_of(t - (z - 1))

        @pl.when(valid & (z > 0) & (rising >= z))
        def _():
            take(rising, rising, pc)

            @pl.when(rising > z)
            def _():
                send_up(rising, pc).start()

        mirrored, pd, due = turn_of(t - (nz - 2 - z))
        falling = nz - 1 - mirrored

        @pl.when(due & (z < nz - 1) & (falling <= z))
        def _():
            take(jnp.where(falling == z, nz, falling), falling, pd)

            @pl.when(falling < z)
            def _():
                send_down(falling, pd).start()

    def relay(j):
        for s in range(1, bits):
            for m in order:
                for q in range(pieces):
                    if m and sent_at(m, q % parts) == s:
                        total = arrived(j, m, q, s).astype(BF16)
                        tb[j, tile_rows(m, q), :] = total
                        d_copy(j, m, q).start()

    def shared_store(j):
        return pltpu.make_async_copy(shv.at[j], shared_out.at[:, cols(j)], out_sem.at[j])

    spread = PIECES // 2

    def tail_step(t, carry):
        hop(t)
        mark = t - (PIECES - 1)

        @pl.when((mark >= 0) & (lax.rem(mark, spread) == 0) & (mark < spread * CHUNKS))
        def _():
            relay(lax.div(mark, spread))

        return carry

    lax.fori_loop(0, max(hops + nz - 2, PIECES - 1 + spread * CHUNKS), tail_step, 0)

    def in_store(pc):
        return pltpu.make_async_copy(sib.at[z, pc], in_out.at[:, depth_cols(pc)], in_sem.at[pc])

    each_piece(lambda pc: in_store(pc).start())

    def final(j):
        for q in range(pieces):
            shv[j, pl.ds(q * tile, tile), :] = arrived(j, 0, q, bits)
        shared_store(j).start()

    each_chunk(final)

    for j in range(max(0, CHUNKS - 2), CHUNKS):
        for m in range(nd):
            dom_store(j, m).wait()

    def drain_chip(chip, carry):
        for h in range(HALVES):
            slot = x_slot(chip, c, h)

            @pl.when((chip <= z) & (z + 1 < nz))
            def _():
                x_copy(slot, chip, c, h, up_sem, up).wait_send()

            @pl.when((chip >= z) & (z > 0))
            def _():
                x_copy(slot, chip, c, h, down_sem, down).wait_send()

            x_copy(slot, chip, c, h, side_sem, sibling).wait_send()

        def sums(pc):
            @pl.when(chip > z)
            def _():
                send_up(chip, pc).wait_send()

            @pl.when(chip < z)
            def _():
                send_down(chip, pc).wait_send()

        each_piece(sums)
        return carry

    lax.fori_loop(0, nz, drain_chip, 0)

    def drain_g(k, carry):
        each_chunk(lambda j: g_copy(lax.rem(me + k, n), j).wait_send())
        return carry

    lax.fori_loop(1, n, drain_g, 0)

    def drain_d(j):
        for m in range(1, nd):
            for q in range(pieces):
                d_copy(j, m, q).wait_send()
        shared_store(j).wait()

    each_chunk(drain_d)
    each_piece(lambda pc: in_store(pc).wait())


def fused(n, nd, x, g, sw, dw, count):
    rows, depth = x.shape
    width = sw.shape[1]
    nz = n // 2
    total = n * rows
    block = depth // nd
    bits = nd.bit_length() - 1
    tile = min(TILE, block // min(2, bits))
    pieces = block // tile
    cw, pw = width // CHUNKS, depth // PIECES
    any_spec = pl.BlockSpec(memory_space=pl.ANY)
    dma = pltpu.SemaphoreType.DMA
    vmem = pltpu.VMEM
    return pl.pallas_call(
        functools.partial(fused_kernel, n, nd),
        out_shape=(
            jax.ShapeDtypeStruct((block, width), F32),
            jax.ShapeDtypeStruct((depth, width), BF16),
            jax.ShapeDtypeStruct((rows, depth), BF16),
        ),
        in_specs=[any_spec] * 4 + [pl.BlockSpec(memory_space=pltpu.SMEM)],
        out_specs=(any_spec,) * 3,
        scratch_shapes=[
            vmem((total, depth), BF16),
            vmem((total, width), BF16),
            vmem((depth, width), BF16),
            vmem((CHUNKS, depth, cw), BF16),
            vmem((nd - 1, CHUNKS, block, cw), BF16),
            vmem((nz, PIECES, rows, pw), BF16),
            vmem((nz + 1, PIECES, rows, pw), BF16),
            vmem((2, PIECES, 2 * rows, pw), BF16),
            vmem((2, depth, cw), BF16),
            vmem((CHUNKS, block, cw), F32),
            dma((nz, HALVES)),
            dma((nz, HALVES)),
            dma((nz, HALVES)),
            dma((n, HALVES)),
            dma((n, CHUNKS)),
            dma((n, CHUNKS)),
            dma((2,)),
            dma((CHUNKS,)),
            dma((CHUNKS,)),
            dma((nz, PIECES)),
            dma((nz, PIECES)),
            dma((nz, PIECES)),
            dma((nz + 1, PIECES)),
            dma((nd - 1, CHUNKS, pieces)),
            dma((nd - 1, CHUNKS, pieces)),
            dma((CHUNKS, nd)),
            dma((CHUNKS,)),
            dma((PIECES,)),
            pltpu.SemaphoreType.REGULAR((3, nz)),
        ],
        compiler_params=pltpu.CompilerParams(
            collective_id=0, has_side_effects=True, vmem_limit_bytes=63 * 1024 * 1024
        ),
        name="gather_backprop_reduce",
    )(x, g, sw, dw, count)


def store_kernel(count, *refs):
    sources, targets, held = refs[:count], refs[count : 2 * count], refs[2 * count : 3 * count]
    in_sem, out_sem = refs[3 * count :]

    def copies(k):
        for i in range(count):
            step = sources[i].shape[0] // STORES
            at = pl.ds(k * step, step)
            yield (
                pltpu.make_async_copy(sources[i].at[at], held[i].at[at], in_sem.at[i, k]),
                pltpu.make_async_copy(held[i].at[at], targets[i].at[at], out_sem.at[i, k]),
            )

    for k in range(STORES):
        for load, _ in copies(k):
            load.start()
    for k in range(STORES):
        for load, store in copies(k):
            load.wait()
            store.start()
    for k in range(STORES):
        for _, store in copies(k):
            store.wait()


def store_results(*arrays):
    count = len(arrays)
    any_spec = pl.BlockSpec(memory_space=pl.ANY)
    return pl.pallas_call(
        functools.partial(store_kernel, count),
        out_shape=tuple(jax.ShapeDtypeStruct(a.shape, a.dtype) for a in arrays),
        in_specs=[any_spec] * count,
        out_specs=(any_spec,) * count,
        scratch_shapes=[pltpu.VMEM(a.shape, a.dtype) for a in arrays]
        + [pltpu.SemaphoreType.DMA((count, STORES))] * 2,
        compiler_params=pltpu.CompilerParams(vmem_limit_bytes=63 * 1024 * 1024),
        name="store_results",
    )(*arrays)


def solution(mesh):
    n, nd = mesh.shape["fsdp"], mesh.shape["dom"]

    def body(inputs, cotangent, shared_weight, domain_weight, row_counts):
        results = fused(
            n, nd, inputs[0], cotangent[0], shared_weight, domain_weight[0], row_counts
        )
        shared_grad, domain_grad, input_grad = store_results(*results)
        return (shared_grad, domain_grad[None], input_grad[None])

    return jax.shard_map(
        body,
        mesh=mesh,
        in_specs=(
            P("dom", "fsdp", None),
            P("dom", "fsdp", None),
            P(None, "fsdp"),
            P("dom", None, "fsdp"),
            P("dom"),
        ),
        out_specs=(P("dom", "fsdp"), P("dom", None, "fsdp"), P("dom", "fsdp", None)),
        check_vma=False,
    )
```

```python
import functools

import jax
import jax.numpy as jnp
from jax import lax
from jax.experimental import pallas as pl
from jax.experimental.pallas import tpu as pltpu
from jax.sharding import PartitionSpec as P

MESH = pl.DeviceIdType.MESH
F32 = jnp.float32
BF16 = jnp.bfloat16
CHUNKS = 4
PIECES = 8
PAIR = 2
HALVES = 2
EARLY = 2
STORES = 8
LAG = 2
TILE = 256


def fused_kernel(
    n, nd, x_ref, g_ref, sw_ref, dw_ref, count_ref, shared_out, dom_out, in_out,
    xs, gs, weff, tb, rb, sib, chain, dxb, swb, shv,
    up_sem, down_sem, side_sem, x_sem, gsend_sem, g_sem, own_sem, sw_sem, dw_sem,
    sib_send, sib_recv, ch_send, ch_recv, d_send, d_recv, dom_sem, out_sem, in_sem, ready,
):
    me, dom = lax.axis_index("fsdp"), lax.axis_index("dom")
    nz = n // 2
    z, c = lax.div(me, 2), lax.rem(me, 2)
    up, down, sibling = me + 2, me - 2, z * 2 + (1 - c)
    rows, depth = x_ref.shape
    width = sw_ref.shape[1]
    cw = width // CHUNKS
    pw = depth // PIECES
    block = depth // nd
    bits = nd.bit_length() - 1
    parts = min(2, bits)
    tile = min(TILE, block // parts)
    pieces = block // tile

    def flip(value, mask):
        for b in range(bits):
            if mask >> b & 1:
                value = value + (1 << b) - (2 << b) * lax.rem(lax.div(value, 1 << b), 2)
        return value

    barrier = pltpu.get_barrier_semaphore()

    def greet(k, carry):
        pl.semaphore_signal(
            barrier, inc=1, device_id={"fsdp": lax.rem(me + k, n)}, device_id_type=MESH
        )
        return carry

    lax.fori_loop(1, n, greet, 0)
    for b in range(bits):
        pl.semaphore_signal(
            barrier, inc=1, device_id={"dom": flip(dom, 1 << b)}, device_id_type=MESH
        )

    def cols(j):
        return pl.ds(pl.multiple_of(j * cw, cw), cw)

    def depth_cols(pc):
        return pl.ds(pl.multiple_of(pc * pw, pw), pw)

    def chip_rows(chip):
        return pl.ds(pl.multiple_of(chip * (2 * rows), 2 * rows), 2 * rows)

    def core_rows(chip, core):
        return pl.ds(pl.multiple_of((chip * 2 + core) * rows, rows), rows)

    def sw_load(j):
        return pltpu.make_async_copy(sw_ref.at[:, cols(j)], swb.at[lax.rem(j, 2)], sw_sem.at[j])

    def dw_load(j):
        return pltpu.make_async_copy(dw_ref.at[:, cols(j)], tb.at[j], dw_sem.at[j])

    own_x = pltpu.make_async_copy(x_ref, xs.at[core_rows(z, c)], own_sem.at[0])
    own_g = pltpu.make_async_copy(
        g_ref.at[:, pl.ds(pl.multiple_of(me * width, width), width)],
        gs.at[core_rows(z, c)],
        own_sem.at[1],
    )
    for j in range(CHUNKS):
        if j < 2:
            sw_load(j).start()
        dw_load(j).start()
    own_x.start()
    own_g.start()

    pl.semaphore_wait(barrier, n - 1 + bits)

    part = rows // HALVES

    def x_slot(chip, core, h):
        at = (chip * 2 + core) * rows + h * part
        return xs.at[pl.ds(pl.multiple_of(at, part), part)]

    def x_copy(src, chip, core, h, sem, target):
        return pltpu.make_async_remote_copy(
            src_ref=src,
            dst_ref=x_slot(chip, core, h),
            send_sem=sem.at[chip, h],
            recv_sem=x_sem.at[chip * 2 + core, h],
            device_id={"fsdp": target},
            device_id_type=MESH,
        )

    def g_copy(target, j):
        at = pl.ds(pl.multiple_of(target * width + j * cw, cw), cw)
        return pltpu.make_async_remote_copy(
            src_ref=g_ref.at[:, at],
            dst_ref=gs.at[core_rows(z, c), cols(j)],
            send_sem=gsend_sem.at[target, j],
            recv_sem=g_sem.at[me, j],
            device_id={"fsdp": target},
            device_id_type=MESH,
        )

    for h in range(HALVES):
        mine = x_ref.at[pl.ds(h * part, part)]

        @pl.when(z + 1 < nz)
        def _():
            x_copy(mine, z, c, h, up_sem, up).start()

        @pl.when(z > 0)
        def _():
            x_copy(mine, z, c, h, down_sem, down).start()

        x_copy(mine, z, c, h, side_sem, sibling).start()

    def each_chunk(body):
        def step(j, carry):
            body(j)
            return carry

        lax.fori_loop(0, CHUNKS, step, 0)

    each_chunk(lambda j: g_copy(sibling, j).start())

    def send_g_near(chip):
        def one(j):
            for core in range(2):
                g_copy(chip * 2 + core, j).start()

        each_chunk(one)

    def is_end(chip):
        return (chip == 0) | (chip == nz - 1)

    def is_far(chip):
        return (chip >= 0) & (chip < nz) & ((chip > z + 1) | (chip < z - 1))

    def send_g_middle(j):
        def one(chip, carry):
            @pl.when(is_far(chip))
            def _():
                for core in range(2):
                    g_copy(chip * 2 + core, j).start()

            return carry

        lax.fori_loop(1, nz - 1, one, 0)

    def send_g_end(level):
        for chip in (0, nz - 1):
            across = is_end(z)
            mine = jnp.logical_not(across) if level == 2 else True

            @pl.when(is_far(chip) & mine)
            def _():
                pl.semaphore_wait(ready.at[level, chip], 2)

                def one(j, carry):
                    for core in range(2):
                        g_copy(chip * 2 + core, j).start()
                    return carry

                until = (1, jnp.where(across, CHUNKS, 2), CHUNKS)[level]
                lax.fori_loop(level, until, one, 0)

    def tell_far(level):
        def one(chip, carry):
            theirs = jnp.logical_not(is_end(chip)) if level == 2 else True

            @pl.when(is_far(chip) & theirs)
            def _():
                for core in range(2):
                    pl.semaphore_signal(
                        ready.at[level, z],
                        inc=1,
                        device_id={"fsdp": chip * 2 + core},
                        device_id_type=MESH,
                    )

            return carry

        @pl.when(is_end(z))
        def _():
            lax.fori_loop(0, nz, one, 0)

    et = min(512, depth)

    def make_weff(j):
        sw_load(j).wait()
        dw_load(j).wait()

        def one(i, carry):
            at = pl.ds(pl.multiple_of(i * et, et), et)
            weff[at, cols(j)] = (
                swb[lax.rem(j, 2), at, :].astype(F32) * tb[j, at, :].astype(F32)
            ).astype(BF16)
            return carry

        lax.fori_loop(0, depth // et, one, 0)

        @pl.when(j + 2 < CHUNKS)
        def _():
            sw_load(j + 2).start()

    each_chunk(make_weff)
    for j in range(2):
        sw_load(j).start()
    own_x.wait()
    own_g.wait()

    count = count_ref[0]
    scale = lax.rsqrt(jnp.full((1, 1), count, jnp.int32).astype(F32))

    def wait_x_half(chip, core, h):
        slot = x_slot(chip, core, h)
        x_copy(slot, chip, core, h, side_sem, sibling).wait_recv()

    def wait_x(chip, core):
        for h in range(HALVES):
            wait_x_half(chip, core, h)

    def wait_g(chip, core, j):
        pltpu.make_async_remote_copy(
            src_ref=gs.at[core_rows(chip, core), cols(j)],
            dst_ref=gs.at[core_rows(chip, core), cols(j)],
            send_sem=gsend_sem.at[me, j],
            recv_sem=g_sem.at[chip * 2 + core, j],
            device_id={"fsdp": sibling},
            device_id_type=MESH,
        ).wait_recv()

    def pre(chip, j):
        wait_g(chip, 1 - c, j)

        @pl.when(chip != z)
        def _():
            wait_g(chip, c, j)

        here = chip_rows(chip)
        preact = jnp.dot(xs[here, :], weff[:, cols(j)], preferred_element_type=F32)
        sigma = jax.nn.sigmoid(preact)
        position = chip * (2 * rows) + lax.broadcasted_iota(jnp.int32, preact.shape, 0)
        slope = gs[here, cols(j)].astype(F32) * sigma * (1.0 + preact * (1.0 - sigma))
        gs[here, cols(j)] = jnp.where(position < count, slope, 0.0).astype(BF16)

    def sib_copy(chip, slot, pc):
        return pltpu.make_async_remote_copy(
            src_ref=dxb.at[slot, pc, pl.ds(pl.multiple_of((1 - c) * rows, rows), rows)],
            dst_ref=sib.at[chip, pc],
            send_sem=sib_send.at[chip, pc],
            recv_sem=sib_recv.at[chip, pc],
            device_id={"fsdp": sibling},
            device_id_type=MESH,
        )

    def chain_copy(slot, chip, pc, target):
        return pltpu.make_async_remote_copy(
            src_ref=sib.at[chip, pc],
            dst_ref=chain.at[slot, pc],
            send_sem=ch_send.at[chip, pc],
            recv_sem=ch_recv.at[slot, pc],
            device_id={"fsdp": target},
            device_id_type=MESH,
        )

    def send_up(chip, pc):
        return chain_copy(chip, chip, pc, lax.rem(me + 2, n))

    def send_down(chip, pc):
        return chain_copy(jnp.where(chip == z - 1, nz, chip), chip, pc, lax.rem(me + n - 2, n))

    def pair_sum(chip, slot, pc):
        sib_copy(chip, slot, pc).wait_send()
        sib_copy(chip, slot, pc).wait_recv()
        own = dxb[slot, pc, pl.ds(pl.multiple_of(c * rows, rows), rows), :]
        sib[chip, pc] = (own.astype(F32) + sib[chip, pc].astype(F32)).astype(BF16)

        @pl.when((z == 0) & (chip > z))
        def _():
            send_up(chip, pc).start()

        @pl.when((z == nz - 1) & (chip < z))
        def _():
            send_down(chip, pc).start()

    def each_piece(body):
        def step(pc, carry):
            body(pc)
            return carry

        lax.fori_loop(0, PIECES, step, 0)

    def back(chip, turn, before, pending):
        slot = lax.rem(turn, 2)

        def one(group, carry):
            wide = PAIR * pw
            at = pl.ds(pl.multiple_of(group * wide, wide), wide)
            partial = lax.dot_general(
                gs[chip_rows(chip), :],
                weff[at, :],
                (((1,), (1,)), ((), ())),
                preferred_element_type=F32,
            ).astype(BF16)
            for i in range(PAIR):
                pc = group * PAIR + i
                dxb[slot, pc] = partial[:, i * pw : (i + 1) * pw]
                sib_copy(chip, slot, pc).start()

            @pl.when(pending)
            def _():
                for i in range(PAIR):
                    pair_sum(before, 1 - slot, group * PAIR + i)

            return carry

        lax.fori_loop(0, PIECES // PAIR, one, 0)

    wait_x(z, 1 - c)
    each_chunk(lambda j: pre(z, j))
    back(z, 0, z, False)

    def receive(chip, h, forward, target, sem):
        wait_x_half(chip, c, h)
        slot = x_slot(chip, c, h)

        @pl.when(forward)
        def _():
            x_copy(slot, chip, c, h, sem, target).start()

        x_copy(slot, chip, c, h, side_sem, sibling).start()

    def receive_both(distance, h):
        below, above = z - distance, z + distance

        @pl.when(below >= 0)
        def _():
            receive(below, h, z + 1 < nz, up, up_sem)

        @pl.when(above < nz)
        def _():
            receive(above, h, z > 0, down, down_sem)

    @pl.when(z == 0)
    def _():
        send_g_near(z + 1)

    @pl.when(z == nz - 1)
    def _():
        send_g_near(z - 1)

    def gather_step(distance, carry):
        for h in range(HALVES):
            receive_both(distance, h)

        @pl.when((distance == 1) & (z > 0) & (z < nz - 1))
        def _():
            send_g_near(z + 1)
            send_g_near(z - 1)

        @pl.when(distance == nz - 2)
        def _():
            each_chunk(send_g_middle)

        return carry

    lax.fori_loop(1, nz - 1, gather_step, 0)

    def near(side, carry):
        turn, before = carry
        chip = z - 1 + 2 * side
        valid = (chip >= 0) & (chip < nz)

        @pl.when(valid)
        def _():
            wait_x(chip, 1 - c)
            each_chunk(lambda j: pre(chip, j))
            back(chip, turn, before, True)

        return jnp.where(valid, turn + 1, turn), jnp.where(valid, chip, before)

    turns, last = lax.fori_loop(0, 2, near, (1, z))

    def flush(chip, turn, first, last):
        def one(pc, carry):
            pair_sum(chip, lax.rem(turn, 2), pc)
            return carry

        lax.fori_loop(first, last, one, 0)

    flush(last, turns - 1, 0, PIECES // 4)
    for h in range(HALVES):
        receive_both(nz - 1, h)
        if h == 0:
            tell_far(0)
            send_g_end(0)
            flush(last, turns - 1, PIECES // 4, PIECES)
    tell_far(1)

    @pl.when(is_end(z))
    def _():
        send_g_end(1)

    farthest = jnp.where(z < nz // 2, nz - 1, 0)

    def each_far(body):
        def one(k, carry):
            chip = jnp.where(z < nz // 2, nz - 1 - k, k)
            return body(chip, is_far(chip), carry)

        return lambda carry: lax.fori_loop(0, nz, one, carry)

    order = sorted(range(nd), key=lambda m: (-bin(m).count("1"), m))

    def bit_order(p):
        return [(p + s) % bits for s in range(bits)]

    def sent_at(m, p):
        return next((s for s, b in enumerate(bit_order(p)) if m >> b & 1), bits)

    index = [{} for _ in range(parts)]
    for p in range(parts):
        for m in range(1, nd):
            s = sent_at(m, p)
            index[p][s, m ^ (1 << bit_order(p)[s])] = len(index[p])

    def tile_rows(m, q):
        return pl.ds(pl.multiple_of(flip(dom, m) * block + q * tile, tile), tile)

    def block_rows(m):
        return pl.ds(pl.multiple_of(flip(dom, m) * block, block), block)

    def d_copy(j, m, q):
        p = q % parts
        s = sent_at(m, p)
        bit = 1 << bit_order(p)[s]
        at = index[p][s, m ^ bit]
        return pltpu.make_async_remote_copy(
            src_ref=tb.at[j, tile_rows(m, q)],
            dst_ref=rb.at[at, j, pl.ds(q * tile, tile)],
            send_sem=d_send.at[at, j, q],
            recv_sem=d_recv.at[at, j, q],
            device_id={"dom": flip(dom, bit)},
            device_id_type=MESH,
        )

    def arrived(j, m, q, steps):
        p = q % parts
        total = tb[j, tile_rows(m, q), :].astype(F32)
        for s in range(steps):
            at = index[p][s, m]
            here = pl.ds(q * tile, tile)
            pltpu.make_async_remote_copy(
                src_ref=rb.at[at, j, here],
                dst_ref=rb.at[at, j, here],
                send_sem=d_send.at[at, j, q],
                recv_sem=d_recv.at[at, j, q],
                device_id={"dom": flip(dom, 1 << bit_order(p)[s])},
                device_id_type=MESH,
            ).wait_recv()
            total = total + rb[at, j, here, :].astype(F32)
        return total

    def dom_store(j, m):
        return pltpu.make_async_copy(
            swb.at[lax.rem(j, 2), block_rows(m)],
            dom_out.at[block_rows(m), cols(j)],
            dom_sem.at[j, m],
        )

    def weight_chunk(j):
        sw_load(j).wait()

        @pl.when((j >= 1) & (j + 1 < CHUNKS))
        def _():
            for m in range(nd):
                dom_store(j - 1, m).wait()
            sw_load(j + 1).start()

        slot = lax.rem(j, 2)
        for m in order:
            at = block_rows(m)
            scaled = scale * lax.dot_general(
                xs[:, at], gs[:, cols(j)], (((0,), (0,)), ((), ())), preferred_element_type=F32
            )
            tb[j, at, :] = (scaled * tb[j, at, :].astype(F32)).astype(BF16)
            for q in range(pieces):
                if sent_at(m, q % parts) == 0:
                    d_copy(j, m, q).start()
            swb[slot, at, :] = (scaled * swb[slot, at, :].astype(F32)).astype(BF16)
            dom_store(j, m).start()

    def wait_far_x(chip, valid, carry):
        @pl.when(valid)
        def _():
            wait_x(chip, 1 - c)

        return carry

    each_far(wait_far_x)(0)

    def chunk_step(j):
        @pl.when((j == 1) & (z > 0) & (z < nz - 1))
        def _():
            send_g_end(1)

        @pl.when((j == 2) & (z > 0) & (z < nz - 1))
        def _():
            send_g_end(2)

        @pl.when(j <= EARLY)
        def _():
            def some(i, carry):
                pre(farthest, i)
                return carry

            lax.fori_loop(j, jnp.where(j == EARLY, CHUNKS, j + 1), some, 0)

        @pl.when(j == 0)
        def _():
            tell_far(2)

        @pl.when(j == EARLY)
        def _():
            back(farthest, turns, farthest, False)
            flush(farthest, turns, 0, PIECES)

        def far_pre(chip, valid, carry):
            @pl.when(valid & (chip != farthest))
            def _():
                pre(chip, j)

            return carry

        each_far(far_pre)(0)

        @pl.when(j == CHUNKS - 1)
        def _():
            def far_back(chip, valid, carry):
                turn, before, pending = carry
                new = valid & (chip != farthest)

                @pl.when(new)
                def _():
                    back(chip, turn, before, pending > 0)

                return (
                    jnp.where(new, turn + 1, turn),
                    jnp.where(new, chip, before),
                    jnp.where(new, 1, pending),
                )

            turn, before, pending = each_far(far_back)((turns + 1, farthest, 0))

            @pl.when(pending > 0)
            def _():
                flush(before, turn - 1, 0, PIECES)

        weight_chunk(j)

    each_chunk(chunk_step)

    hops = (nz - 1) * PIECES

    def take(slot, chip, pc):
        pltpu.make_async_remote_copy(
            src_ref=chain.at[slot, pc],
            dst_ref=chain.at[slot, pc],
            send_sem=ch_send.at[chip, pc],
            recv_sem=ch_recv.at[slot, pc],
            device_id={"fsdp": sibling},
            device_id_type=MESH,
        ).wait_recv()
        sib[chip, pc] = (sib[chip, pc].astype(F32) + chain[slot, pc].astype(F32)).astype(BF16)

    def turn_of(step):
        turn = lax.div(step, PIECES)
        rising = jnp.where(turn == 0, 1, nz - turn)
        return rising, lax.rem(step, PIECES), (step >= 0) & (step < hops)

    def hop(t):
        rising, pc, valid = turn_of(t - LAG * (z - 1))

        @pl.when(valid & (z > 0) & (rising >= z))
        def _():
            take(rising, rising, pc)

            @pl.when(rising > z)
            def _():
                send_up(rising, pc).start()

        mirrored, pd, due = turn_of(t - LAG * (nz - 2 - z))
        falling = nz - 1 - mirrored

        @pl.when(due & (z < nz - 1) & (falling <= z))
        def _():
            take(jnp.where(falling == z, nz, falling), falling, pd)

            @pl.when(falling < z)
            def _():
                send_down(falling, pd).start()

    def relay(j):
        for s in range(1, bits):
            for m in order:
                for q in range(pieces):
                    if m and sent_at(m, q % parts) == s:
                        total = arrived(j, m, q, s).astype(BF16)
                        tb[j, tile_rows(m, q), :] = total
                        d_copy(j, m, q).start()

    def shared_store(j):
        return pltpu.make_async_copy(shv.at[j], shared_out.at[:, cols(j)], out_sem.at[j])

    spread = PIECES // 2

    def tail_step(t, carry):
        hop(t)
        mark = t - (PIECES - 1)

        @pl.when((mark >= 0) & (lax.rem(mark, spread) == 0) & (mark < spread * CHUNKS))
        def _():
            relay(lax.div(mark, spread))

        return carry

    lax.fori_loop(0, max(hops + LAG * (nz - 2), PIECES - 1 + spread * CHUNKS), tail_step, 0)

    def in_store(pc):
        return pltpu.make_async_copy(sib.at[z, pc], in_out.at[:, depth_cols(pc)], in_sem.at[pc])

    each_piece(lambda pc: in_store(pc).start())

    def final(j):
        for q in range(pieces):
            shv[j, pl.ds(q * tile, tile), :] = arrived(j, 0, q, bits)
        shared_store(j).start()

    each_chunk(final)

    for j in range(max(0, CHUNKS - 2), CHUNKS):
        for m in range(nd):
            dom_store(j, m).wait()

    def drain_chip(chip, carry):
        for h in range(HALVES):
            slot = x_slot(chip, c, h)

            @pl.when((chip <= z) & (z + 1 < nz))
            def _():
                x_copy(slot, chip, c, h, up_sem, up).wait_send()

            @pl.when((chip >= z) & (z > 0))
            def _():
                x_copy(slot, chip, c, h, down_sem, down).wait_send()

            x_copy(slot, chip, c, h, side_sem, sibling).wait_send()

        def sums(pc):
            @pl.when(chip > z)
            def _():
                send_up(chip, pc).wait_send()

            @pl.when(chip < z)
            def _():
                send_down(chip, pc).wait_send()

        each_piece(sums)
        return carry

    lax.fori_loop(0, nz, drain_chip, 0)

    def drain_g(k, carry):
        each_chunk(lambda j: g_copy(lax.rem(me + k, n), j).wait_send())
        return carry

    lax.fori_loop(1, n, drain_g, 0)

    def drain_d(j):
        for m in range(1, nd):
            for q in range(pieces):
                d_copy(j, m, q).wait_send()
        shared_store(j).wait()

    each_chunk(drain_d)
    each_piece(lambda pc: in_store(pc).wait())


def fused(n, nd, x, g, sw, dw, count):
    rows, depth = x.shape
    width = sw.shape[1]
    nz = n // 2
    total = n * rows
    block = depth // nd
    bits = nd.bit_length() - 1
    tile = min(TILE, block // min(2, bits))
    pieces = block // tile
    cw, pw = width // CHUNKS, depth // PIECES
    any_spec = pl.BlockSpec(memory_space=pl.ANY)
    dma = pltpu.SemaphoreType.DMA
    vmem = pltpu.VMEM
    return pl.pallas_call(
        functools.partial(fused_kernel, n, nd),
        out_shape=(
            jax.ShapeDtypeStruct((block, width), F32),
            jax.ShapeDtypeStruct((depth, width), BF16),
            jax.ShapeDtypeStruct((rows, depth), BF16),
        ),
        in_specs=[any_spec] * 4 + [pl.BlockSpec(memory_space=pltpu.SMEM)],
        out_specs=(any_spec,) * 3,
        scratch_shapes=[
            vmem((total, depth), BF16),
            vmem((total, width), BF16),
            vmem((depth, width), BF16),
            vmem((CHUNKS, depth, cw), BF16),
            vmem((nd - 1, CHUNKS, block, cw), BF16),
            vmem((nz, PIECES, rows, pw), BF16),
            vmem((nz + 1, PIECES, rows, pw), BF16),
            vmem((2, PIECES, 2 * rows, pw), BF16),
            vmem((2, depth, cw), BF16),
            vmem((CHUNKS, block, cw), F32),
            dma((nz, HALVES)),
            dma((nz, HALVES)),
            dma((nz, HALVES)),
            dma((n, HALVES)),
            dma((n, CHUNKS)),
            dma((n, CHUNKS)),
            dma((2,)),
            dma((CHUNKS,)),
            dma((CHUNKS,)),
            dma((nz, PIECES)),
            dma((nz, PIECES)),
            dma((nz, PIECES)),
            dma((nz + 1, PIECES)),
            dma((nd - 1, CHUNKS, pieces)),
            dma((nd - 1, CHUNKS, pieces)),
            dma((CHUNKS, nd)),
            dma((CHUNKS,)),
            dma((PIECES,)),
            pltpu.SemaphoreType.REGULAR((3, nz)),
        ],
        compiler_params=pltpu.CompilerParams(
            collective_id=0, has_side_effects=True, vmem_limit_bytes=63 * 1024 * 1024
        ),
        name="gather_backprop_reduce",
    )(x, g, sw, dw, count)


def store_kernel(count, *refs):
    sources, targets, held = refs[:count], refs[count : 2 * count], refs[2 * count : 3 * count]
    in_sem, out_sem = refs[3 * count :]

    def copies(k):
        for i in range(count):
            step = sources[i].shape[0] // STORES
            at = pl.ds(k * step, step)
            yield (
                pltpu.make_async_copy(sources[i].at[at], held[i].at[at], in_sem.at[i, k]),
                pltpu.make_async_copy(held[i].at[at], targets[i].at[at], out_sem.at[i, k]),
            )

    for k in range(STORES):
        for load, _ in copies(k):
            load.start()
    for k in range(STORES):
        for load, store in copies(k):
            load.wait()
            store.start()
    for k in range(STORES):
        for _, store in copies(k):
            store.wait()


def store_results(*arrays):
    count = len(arrays)
    any_spec = pl.BlockSpec(memory_space=pl.ANY)
    return pl.pallas_call(
        functools.partial(store_kernel, count),
        out_shape=tuple(jax.ShapeDtypeStruct(a.shape, a.dtype) for a in arrays),
        in_specs=[any_spec] * count,
        out_specs=(any_spec,) * count,
        scratch_shapes=[pltpu.VMEM(a.shape, a.dtype) for a in arrays]
        + [pltpu.SemaphoreType.DMA((count, STORES))] * 2,
        compiler_params=pltpu.CompilerParams(vmem_limit_bytes=63 * 1024 * 1024),
        name="store_results",
    )(*arrays)


def solution(mesh):
    n, nd = mesh.shape["fsdp"], mesh.shape["dom"]

    def body(inputs, cotangent, shared_weight, domain_weight, row_counts):
        results = fused(
            n, nd, inputs[0], cotangent[0], shared_weight, domain_weight[0], row_counts
        )
        shared_grad, domain_grad, input_grad = store_results(*results)
        return (shared_grad, domain_grad[None], input_grad[None])

    return jax.shard_map(
        body,
        mesh=mesh,
        in_specs=(
            P("dom", "fsdp", None),
            P("dom", "fsdp", None),
            P(None, "fsdp"),
            P("dom", None, "fsdp"),
            P("dom"),
        ),
        out_specs=(P("dom", "fsdp"), P("dom", None, "fsdp"), P("dom", "fsdp", None)),
        check_vma=False,
    )
```

```python
import functools

import jax
import jax.numpy as jnp
from jax import lax
from jax.experimental import pallas as pl
from jax.experimental.pallas import tpu as pltpu
from jax.sharding import PartitionSpec as P

MESH = pl.DeviceIdType.MESH
F32 = jnp.float32
BF16 = jnp.bfloat16
CHUNKS = 4
PIECES = 8
PAIR = 2
HALVES = 2
EARLY = 2
STORES = 8
LIMIT = 63 * 1024 * 1024
LAG = 2
TILE = 256


def fused_kernel(
    n, nd, x_ref, g_ref, sw_ref, dw_ref, count_ref, shared_out, dom_out, in_out,
    xs, gs, weff, tb, rb, sib, chain, dxb,
    up_sem, down_sem, side_sem, x_sem, gsend_sem, g_sem, own_sem, sw_sem, dw_sem,
    sib_send, sib_recv, ch_send, ch_recv, d_send, d_recv, ready,
):
    me, dom = lax.axis_index("fsdp"), lax.axis_index("dom")
    nz = n // 2
    z, c = lax.div(me, 2), lax.rem(me, 2)
    up, down, sibling = me + 2, me - 2, z * 2 + (1 - c)
    rows, depth = x_ref.shape
    width = sw_ref.shape[1]
    cw = width // CHUNKS
    pw = depth // PIECES
    block = depth // nd
    bits = nd.bit_length() - 1
    parts = min(2, bits)
    tile = min(TILE, block // parts)
    pieces = block // tile

    def flip(value, mask):
        for b in range(bits):
            if mask >> b & 1:
                value = value + (1 << b) - (2 << b) * lax.rem(lax.div(value, 1 << b), 2)
        return value

    barrier = pltpu.get_barrier_semaphore()

    def greet(k, carry):
        pl.semaphore_signal(
            barrier, inc=1, device_id={"fsdp": lax.rem(me + k, n)}, device_id_type=MESH
        )
        return carry

    lax.fori_loop(1, n, greet, 0)
    for b in range(bits):
        pl.semaphore_signal(
            barrier, inc=1, device_id={"dom": flip(dom, 1 << b)}, device_id_type=MESH
        )

    def cols(j):
        return pl.ds(pl.multiple_of(j * cw, cw), cw)

    def depth_cols(pc):
        return pl.ds(pl.multiple_of(pc * pw, pw), pw)

    def chip_rows(chip):
        return pl.ds(pl.multiple_of(chip * (2 * rows), 2 * rows), 2 * rows)

    def core_rows(chip, core):
        return pl.ds(pl.multiple_of((chip * 2 + core) * rows, rows), rows)

    def sw_load(j):
        return pltpu.make_async_copy(sw_ref.at[:, cols(j)], dom_out.at[:, cols(j)], sw_sem.at[j])

    def dw_load(j):
        return pltpu.make_async_copy(dw_ref.at[:, cols(j)], tb.at[j], dw_sem.at[j])

    own_x = pltpu.make_async_copy(x_ref, xs.at[core_rows(z, c)], own_sem.at[0])
    own_g = pltpu.make_async_copy(
        g_ref.at[:, pl.ds(pl.multiple_of(me * width, width), width)],
        gs.at[core_rows(z, c)],
        own_sem.at[1],
    )
    for j in range(CHUNKS):
        sw_load(j).start()
        dw_load(j).start()
    own_x.start()
    own_g.start()

    pl.semaphore_wait(barrier, n - 1 + bits)

    part = rows // HALVES

    def x_slot(chip, core, h):
        at = (chip * 2 + core) * rows + h * part
        return xs.at[pl.ds(pl.multiple_of(at, part), part)]

    def x_copy(src, chip, core, h, sem, target):
        return pltpu.make_async_remote_copy(
            src_ref=src,
            dst_ref=x_slot(chip, core, h),
            send_sem=sem.at[chip, h],
            recv_sem=x_sem.at[chip * 2 + core, h],
            device_id={"fsdp": target},
            device_id_type=MESH,
        )

    def g_copy(target, j):
        at = pl.ds(pl.multiple_of(target * width + j * cw, cw), cw)
        return pltpu.make_async_remote_copy(
            src_ref=g_ref.at[:, at],
            dst_ref=gs.at[core_rows(z, c), cols(j)],
            send_sem=gsend_sem.at[target, j],
            recv_sem=g_sem.at[me, j],
            device_id={"fsdp": target},
            device_id_type=MESH,
        )

    for h in range(HALVES):
        mine = x_ref.at[pl.ds(h * part, part)]

        @pl.when(z + 1 < nz)
        def _():
            x_copy(mine, z, c, h, up_sem, up).start()

        @pl.when(z > 0)
        def _():
            x_copy(mine, z, c, h, down_sem, down).start()

        x_copy(mine, z, c, h, side_sem, sibling).start()

    def each_chunk(body):
        def step(j, carry):
            body(j)
            return carry

        lax.fori_loop(0, CHUNKS, step, 0)

    each_chunk(lambda j: g_copy(sibling, j).start())

    def send_g_near(chip):
        def one(j):
            for core in range(2):
                g_copy(chip * 2 + core, j).start()

        each_chunk(one)

    def is_end(chip):
        return (chip == 0) | (chip == nz - 1)

    def is_far(chip):
        return (chip >= 0) & (chip < nz) & ((chip > z + 1) | (chip < z - 1))

    def send_g_middle(j):
        def one(chip, carry):
            @pl.when(is_far(chip))
            def _():
                for core in range(2):
                    g_copy(chip * 2 + core, j).start()

            return carry

        lax.fori_loop(1, nz - 1, one, 0)

    def send_g_end(level):
        for chip in (0, nz - 1):
            across = is_end(z)
            mine = jnp.logical_not(across) if level == 2 else True

            @pl.when(is_far(chip) & mine)
            def _():
                pl.semaphore_wait(ready.at[level, chip], 2)

                def one(j, carry):
                    for core in range(2):
                        g_copy(chip * 2 + core, j).start()
                    return carry

                until = (1, jnp.where(across, CHUNKS, 2), CHUNKS)[level]
                lax.fori_loop(level, until, one, 0)

    def tell_far(level):
        def one(chip, carry):
            theirs = jnp.logical_not(is_end(chip)) if level == 2 else True

            @pl.when(is_far(chip) & theirs)
            def _():
                for core in range(2):
                    pl.semaphore_signal(
                        ready.at[level, z],
                        inc=1,
                        device_id={"fsdp": chip * 2 + core},
                        device_id_type=MESH,
                    )

            return carry

        @pl.when(is_end(z))
        def _():
            lax.fori_loop(0, nz, one, 0)

    et = min(512, depth)

    def make_weff(j):
        sw_load(j).wait()
        dw_load(j).wait()

        def one(i, carry):
            at = pl.ds(pl.multiple_of(i * et, et), et)
            weff[at, cols(j)] = (
                dom_out[at, cols(j)].astype(F32) * tb[j, at, :].astype(F32)
            ).astype(BF16)
            return carry

        lax.fori_loop(0, depth // et, one, 0)

    each_chunk(make_weff)
    own_x.wait()
    own_g.wait()

    count = count_ref[0]
    scale = lax.rsqrt(jnp.full((1, 1), count, jnp.int32).astype(F32))

    def wait_x_half(chip, core, h):
        slot = x_slot(chip, core, h)
        x_copy(slot, chip, core, h, side_sem, sibling).wait_recv()

    def wait_x(chip, core):
        for h in range(HALVES):
            wait_x_half(chip, core, h)

    def wait_g(chip, core, j):
        pltpu.make_async_remote_copy(
            src_ref=gs.at[core_rows(chip, core), cols(j)],
            dst_ref=gs.at[core_rows(chip, core), cols(j)],
            send_sem=gsend_sem.at[me, j],
            recv_sem=g_sem.at[chip * 2 + core, j],
            device_id={"fsdp": sibling},
            device_id_type=MESH,
        ).wait_recv()

    def pre(chip, j):
        wait_g(chip, 1 - c, j)

        @pl.when(chip != z)
        def _():
            wait_g(chip, c, j)

        here = chip_rows(chip)
        preact = jnp.dot(xs[here, :], weff[:, cols(j)], preferred_element_type=F32)
        sigma = jax.nn.sigmoid(preact)
        position = chip * (2 * rows) + lax.broadcasted_iota(jnp.int32, preact.shape, 0)
        slope = gs[here, cols(j)].astype(F32) * sigma * (1.0 + preact * (1.0 - sigma))
        gs[here, cols(j)] = jnp.where(position < count, slope, 0.0).astype(BF16)

    def sib_copy(chip, slot, pc):
        return pltpu.make_async_remote_copy(
            src_ref=dxb.at[slot, pc, pl.ds(pl.multiple_of((1 - c) * rows, rows), rows)],
            dst_ref=sib.at[chip, pc],
            send_sem=sib_send.at[chip, pc],
            recv_sem=sib_recv.at[chip, pc],
            device_id={"fsdp": sibling},
            device_id_type=MESH,
        )

    def chain_copy(slot, chip, pc, target):
        return pltpu.make_async_remote_copy(
            src_ref=sib.at[chip, pc],
            dst_ref=chain.at[slot, pc],
            send_sem=ch_send.at[chip, pc],
            recv_sem=ch_recv.at[slot, pc],
            device_id={"fsdp": target},
            device_id_type=MESH,
        )

    def send_up(chip, pc):
        return chain_copy(chip, chip, pc, lax.rem(me + 2, n))

    def send_down(chip, pc):
        return chain_copy(jnp.where(chip == z - 1, nz, chip), chip, pc, lax.rem(me + n - 2, n))

    def pair_sum(chip, slot, pc):
        sib_copy(chip, slot, pc).wait_send()
        sib_copy(chip, slot, pc).wait_recv()
        own = dxb[slot, pc, pl.ds(pl.multiple_of(c * rows, rows), rows), :]
        sib[chip, pc] = (own.astype(F32) + sib[chip, pc].astype(F32)).astype(BF16)

        @pl.when((z == 0) & (chip > z))
        def _():
            send_up(chip, pc).start()

        @pl.when((z == nz - 1) & (chip < z))
        def _():
            send_down(chip, pc).start()

    def each_piece(body):
        def step(pc, carry):
            body(pc)
            return carry

        lax.fori_loop(0, PIECES, step, 0)

    def back(chip, turn, before, pending):
        slot = lax.rem(turn, 2)

        def one(group, carry):
            wide = PAIR * pw
            at = pl.ds(pl.multiple_of(group * wide, wide), wide)
            partial = lax.dot_general(
                gs[chip_rows(chip), :],
                weff[at, :],
                (((1,), (1,)), ((), ())),
                preferred_element_type=F32,
            ).astype(BF16)
            for i in range(PAIR):
                pc = group * PAIR + i
                dxb[slot, pc] = partial[:, i * pw : (i + 1) * pw]
                sib_copy(chip, slot, pc).start()

            @pl.when(pending)
            def _():
                for i in range(PAIR):
                    pair_sum(before, 1 - slot, group * PAIR + i)

            return carry

        lax.fori_loop(0, PIECES // PAIR, one, 0)

    wait_x(z, 1 - c)
    each_chunk(lambda j: pre(z, j))
    back(z, 0, z, False)

    def receive(chip, h, forward, target, sem):
        wait_x_half(chip, c, h)
        slot = x_slot(chip, c, h)

        @pl.when(forward)
        def _():
            x_copy(slot, chip, c, h, sem, target).start()

        x_copy(slot, chip, c, h, side_sem, sibling).start()

    def receive_both(distance, h):
        below, above = z - distance, z + distance

        @pl.when(below >= 0)
        def _():
            receive(below, h, z + 1 < nz, up, up_sem)

        @pl.when(above < nz)
        def _():
            receive(above, h, z > 0, down, down_sem)

    @pl.when(z == 0)
    def _():
        send_g_near(z + 1)

    @pl.when(z == nz - 1)
    def _():
        send_g_near(z - 1)

    def gather_step(distance, carry):
        for h in range(HALVES):
            receive_both(distance, h)

        @pl.when((distance == 1) & (z > 0) & (z < nz - 1))
        def _():
            send_g_near(z + 1)
            send_g_near(z - 1)

        @pl.when(distance == nz - 2)
        def _():
            each_chunk(send_g_middle)

        return carry

    lax.fori_loop(1, nz - 1, gather_step, 0)

    def near(side, carry):
        turn, before = carry
        chip = z - 1 + 2 * side
        valid = (chip >= 0) & (chip < nz)

        @pl.when(valid)
        def _():
            wait_x(chip, 1 - c)
            each_chunk(lambda j: pre(chip, j))
            back(chip, turn, before, True)

        return jnp.where(valid, turn + 1, turn), jnp.where(valid, chip, before)

    turns, last = lax.fori_loop(0, 2, near, (1, z))

    def flush(chip, turn, first, last):
        def one(pc, carry):
            pair_sum(chip, lax.rem(turn, 2), pc)
            return carry

        lax.fori_loop(first, last, one, 0)

    flush(last, turns - 1, 0, PIECES // 4)
    for h in range(HALVES):
        receive_both(nz - 1, h)
        if h == 0:
            tell_far(0)
            send_g_end(0)
            flush(last, turns - 1, PIECES // 4, PIECES)
    tell_far(1)

    @pl.when(is_end(z))
    def _():
        send_g_end(1)

    farthest = jnp.where(z < nz // 2, nz - 1, 0)

    def each_far(body):
        def one(k, carry):
            chip = jnp.where(z < nz // 2, nz - 1 - k, k)
            return body(chip, is_far(chip), carry)

        return lambda carry: lax.fori_loop(0, nz, one, carry)

    order = sorted(range(nd), key=lambda m: (-bin(m).count("1"), m))

    def bit_order(p):
        return [(p + s) % bits for s in range(bits)]

    def sent_at(m, p):
        return next((s for s, b in enumerate(bit_order(p)) if m >> b & 1), bits)

    index = [{} for _ in range(parts)]
    for p in range(parts):
        for m in range(1, nd):
            s = sent_at(m, p)
            index[p][s, m ^ (1 << bit_order(p)[s])] = len(index[p])

    def tile_rows(m, q):
        return pl.ds(pl.multiple_of(flip(dom, m) * block + q * tile, tile), tile)

    def block_rows(m):
        return pl.ds(pl.multiple_of(flip(dom, m) * block, block), block)

    def d_copy(j, m, q):
        p = q % parts
        s = sent_at(m, p)
        bit = 1 << bit_order(p)[s]
        at = index[p][s, m ^ bit]
        return pltpu.make_async_remote_copy(
            src_ref=tb.at[j, tile_rows(m, q)],
            dst_ref=rb.at[at, j, pl.ds(q * tile, tile)],
            send_sem=d_send.at[at, j, q],
            recv_sem=d_recv.at[at, j, q],
            device_id={"dom": flip(dom, bit)},
            device_id_type=MESH,
        )

    def arrived(j, m, q, steps):
        p = q % parts
        total = tb[j, tile_rows(m, q), :].astype(F32)
        for s in range(steps):
            at = index[p][s, m]
            here = pl.ds(q * tile, tile)
            pltpu.make_async_remote_copy(
                src_ref=rb.at[at, j, here],
                dst_ref=rb.at[at, j, here],
                send_sem=d_send.at[at, j, q],
                recv_sem=d_recv.at[at, j, q],
                device_id={"dom": flip(dom, 1 << bit_order(p)[s])},
                device_id_type=MESH,
            ).wait_recv()
            total = total + rb[at, j, here, :].astype(F32)
        return total

    def weight_chunk(j):
        for m in order:
            at = block_rows(m)
            scaled = scale * lax.dot_general(
                xs[:, at], gs[:, cols(j)], (((0,), (0,)), ((), ())), preferred_element_type=F32
            )
            tb[j, at, :] = (scaled * tb[j, at, :].astype(F32)).astype(BF16)
            for q in range(pieces):
                if sent_at(m, q % parts) == 0:
                    d_copy(j, m, q).start()
            dom_out[at, cols(j)] = (scaled * dom_out[at, cols(j)].astype(F32)).astype(BF16)

    def wait_far_x(chip, valid, carry):
        @pl.when(valid)
        def _():
            wait_x(chip, 1 - c)

        return carry

    each_far(wait_far_x)(0)

    def chunk_step(j):
        @pl.when((j == 1) & (z > 0) & (z < nz - 1))
        def _():
            send_g_end(1)

        @pl.when((j == 2) & (z > 0) & (z < nz - 1))
        def _():
            send_g_end(2)

        @pl.when(j <= EARLY)
        def _():
            def some(i, carry):
                pre(farthest, i)
                return carry

            lax.fori_loop(j, jnp.where(j == EARLY, CHUNKS, j + 1), some, 0)

        @pl.when(j == 0)
        def _():
            tell_far(2)

        @pl.when(j == EARLY)
        def _():
            back(farthest, turns, farthest, False)
            flush(farthest, turns, 0, PIECES)

        def far_pre(chip, valid, carry):
            @pl.when(valid & (chip != farthest))
            def _():
                pre(chip, j)

            return carry

        each_far(far_pre)(0)

        @pl.when(j == CHUNKS - 1)
        def _():
            def far_back(chip, valid, carry):
                turn, before, pending = carry
                new = valid & (chip != farthest)

                @pl.when(new)
                def _():
                    back(chip, turn, before, pending > 0)

                return (
                    jnp.where(new, turn + 1, turn),
                    jnp.where(new, chip, before),
                    jnp.where(new, 1, pending),
                )

            turn, before, pending = each_far(far_back)((turns + 1, farthest, 0))

            @pl.when(pending > 0)
            def _():
                flush(before, turn - 1, 0, PIECES)

        weight_chunk(j)

    each_chunk(chunk_step)

    hops = (nz - 1) * PIECES

    def take(slot, chip, pc):
        pltpu.make_async_remote_copy(
            src_ref=chain.at[slot, pc],
            dst_ref=chain.at[slot, pc],
            send_sem=ch_send.at[chip, pc],
            recv_sem=ch_recv.at[slot, pc],
            device_id={"fsdp": sibling},
            device_id_type=MESH,
        ).wait_recv()
        sib[chip, pc] = (sib[chip, pc].astype(F32) + chain[slot, pc].astype(F32)).astype(BF16)

    def turn_of(step):
        turn = lax.div(step, PIECES)
        rising = jnp.where(turn == 0, 1, nz - turn)
        return rising, lax.rem(step, PIECES), (step >= 0) & (step < hops)

    def hop(t):
        rising, pc, valid = turn_of(t - LAG * (z - 1))

        @pl.when(valid & (z > 0) & (rising >= z))
        def _():
            take(rising, rising, pc)

            @pl.when(rising > z)
            def _():
                send_up(rising, pc).start()

        mirrored, pd, due = turn_of(t - LAG * (nz - 2 - z))
        falling = nz - 1 - mirrored

        @pl.when(due & (z < nz - 1) & (falling <= z))
        def _():
            take(jnp.where(falling == z, nz, falling), falling, pd)

            @pl.when(falling < z)
            def _():
                send_down(falling, pd).start()

    def relay(j):
        for s in range(1, bits):
            for m in order:
                for q in range(pieces):
                    if m and sent_at(m, q % parts) == s:
                        total = arrived(j, m, q, s).astype(BF16)
                        tb[j, tile_rows(m, q), :] = total
                        d_copy(j, m, q).start()

    spread = PIECES // 2

    def tail_step(t, carry):
        hop(t)
        mark = t - (PIECES - 1)

        @pl.when((mark >= 0) & (lax.rem(mark, spread) == 0) & (mark < spread * CHUNKS))
        def _():
            relay(lax.div(mark, spread))

        return carry

    lax.fori_loop(0, max(hops + LAG * (nz - 2), PIECES - 1 + spread * CHUNKS), tail_step, 0)

    for pc in range(PIECES):
        in_out[:, pc * pw : (pc + 1) * pw] = sib[z, pc]

    def final(j):
        for q in range(pieces):
            shared_out[pl.ds(q * tile, tile), cols(j)] = arrived(j, 0, q, bits)

    each_chunk(final)

    def drain_chip(chip, carry):
        for h in range(HALVES):
            slot = x_slot(chip, c, h)

            @pl.when((chip <= z) & (z + 1 < nz))
            def _():
                x_copy(slot, chip, c, h, up_sem, up).wait_send()

            @pl.when((chip >= z) & (z > 0))
            def _():
                x_copy(slot, chip, c, h, down_sem, down).wait_send()

            x_copy(slot, chip, c, h, side_sem, sibling).wait_send()

        def sums(pc):
            @pl.when(chip > z)
            def _():
                send_up(chip, pc).wait_send()

            @pl.when(chip < z)
            def _():
                send_down(chip, pc).wait_send()

        each_piece(sums)
        return carry

    lax.fori_loop(0, nz, drain_chip, 0)

    def drain_g(k, carry):
        each_chunk(lambda j: g_copy(lax.rem(me + k, n), j).wait_send())
        return carry

    lax.fori_loop(1, n, drain_g, 0)

    def drain_d(j):
        for m in range(1, nd):
            for q in range(pieces):
                d_copy(j, m, q).wait_send()

    each_chunk(drain_d)


def fused(n, nd, x, g, sw, dw, count):
    rows, depth = x.shape
    width = sw.shape[1]
    nz = n // 2
    total = n * rows
    block = depth // nd
    bits = nd.bit_length() - 1
    tile = min(TILE, block // min(2, bits))
    pieces = block // tile
    cw, pw = width // CHUNKS, depth // PIECES
    kept = block * width * 4 + depth * width * 2 + rows * depth * 2
    any_spec = pl.BlockSpec(memory_space=pl.ANY)
    dma = pltpu.SemaphoreType.DMA
    vmem = pltpu.VMEM
    return pl.pallas_call(
        functools.partial(fused_kernel, n, nd),
        out_shape=(
            vmem((block, width), F32),
            vmem((depth, width), BF16),
            vmem((rows, depth), BF16),
        ),
        in_specs=[any_spec] * 4 + [pl.BlockSpec(memory_space=pltpu.SMEM)],
        out_specs=(pl.BlockSpec(memory_space=vmem),) * 3,
        scratch_shapes=[
            vmem((total, depth), BF16),
            vmem((total, width), BF16),
            vmem((depth, width), BF16),
            vmem((CHUNKS, depth, cw), BF16),
            vmem((nd - 1, CHUNKS, block, cw), BF16),
            vmem((nz, PIECES, rows, pw), BF16),
            vmem((nz + 1, PIECES, rows, pw), BF16),
            vmem((2, PIECES, 2 * rows, pw), BF16),
            dma((nz, HALVES)),
            dma((nz, HALVES)),
            dma((nz, HALVES)),
            dma((n, HALVES)),
            dma((n, CHUNKS)),
            dma((n, CHUNKS)),
            dma((2,)),
            dma((CHUNKS,)),
            dma((CHUNKS,)),
            dma((nz, PIECES)),
            dma((nz, PIECES)),
            dma((nz, PIECES)),
            dma((nz + 1, PIECES)),
            dma((nd - 1, CHUNKS, pieces)),
            dma((nd - 1, CHUNKS, pieces)),
            pltpu.SemaphoreType.REGULAR((3, nz)),
        ],
        compiler_params=pltpu.CompilerParams(
            collective_id=0, has_side_effects=True, vmem_limit_bytes=LIMIT - kept
        ),
        name="gather_backprop_reduce",
    )(x, g, sw, dw, count)


def store_kernel(count, *refs):
    sources, targets, sem = refs[:count], refs[count : 2 * count], refs[2 * count]
    copies = []
    for i in range(count):
        step = sources[i].shape[0] // STORES
        for k in range(STORES):
            at = pl.ds(k * step, step)
            copies.append(pltpu.make_async_copy(sources[i].at[at], targets[i].at[at], sem.at[i, k]))
    for copy in copies:
        copy.start()
    for copy in copies:
        copy.wait()


def store_results(*arrays):
    count = len(arrays)
    return pl.pallas_call(
        functools.partial(store_kernel, count),
        out_shape=tuple(jax.ShapeDtypeStruct(a.shape, a.dtype) for a in arrays),
        in_specs=[pl.BlockSpec(memory_space=pltpu.VMEM)] * count,
        out_specs=(pl.BlockSpec(memory_space=pl.ANY),) * count,
        scratch_shapes=[pltpu.SemaphoreType.DMA((count, STORES))],
        compiler_params=pltpu.CompilerParams(vmem_limit_bytes=16 * 1024 * 1024),
        name="store_results",
    )(*arrays)


def solution(mesh):
    n, nd = mesh.shape["fsdp"], mesh.shape["dom"]

    def body(inputs, cotangent, shared_weight, domain_weight, row_counts):
        results = fused(
            n, nd, inputs[0], cotangent[0], shared_weight, domain_weight[0], row_counts
        )
        results = [pltpu.with_memory_space_constraint(a, pltpu.VMEM) for a in results]
        shared_grad, domain_grad, input_grad = store_results(*results)
        return (shared_grad, domain_grad[None], input_grad[None])

    return jax.shard_map(
        body,
        mesh=mesh,
        in_specs=(
            P("dom", "fsdp", None),
            P("dom", "fsdp", None),
            P(None, "fsdp"),
            P("dom", None, "fsdp"),
            P("dom"),
        ),
        out_specs=(P("dom", "fsdp"), P("dom", None, "fsdp"), P("dom", "fsdp", None)),
        check_vma=False,
    )
```

```python
import functools

import jax
import jax.numpy as jnp
from jax import lax
from jax.experimental import pallas as pl
from jax.experimental.pallas import tpu as pltpu
from jax.sharding import PartitionSpec as P

MESH = pl.DeviceIdType.MESH
F32 = jnp.float32
BF16 = jnp.bfloat16
CHUNKS = 4
PIECES = 8
PAIR = 2
HALVES = 2
EARLY = 2
STORES = 8
LIMIT = 63 * 1024 * 1024
LAG = 2
TILE = 256


def fused_kernel(
    n, nd, x_ref, g_ref, sw_ref, dw_ref, count_ref, shared_out, dom_out, in_out,
    xs, gs, weff, tb, rb, sib, chain, dxb,
    up_sem, down_sem, side_sem, x_sem, gsend_sem, g_sem, own_sem, sw_sem, dw_sem,
    sib_send, sib_recv, ch_send, ch_recv, d_send, d_recv, ready,
):
    me, dom = lax.axis_index("fsdp"), lax.axis_index("dom")
    nz = n // 2
    z, c = lax.div(me, 2), lax.rem(me, 2)
    up, down, sibling = me + 2, me - 2, z * 2 + (1 - c)
    rows, depth = x_ref.shape
    width = sw_ref.shape[1]
    cw = width // CHUNKS
    pw = depth // PIECES
    block = depth // nd
    bits = nd.bit_length() - 1
    parts = min(2, bits)
    tile = min(TILE, block // parts)
    pieces = block // tile

    def flip(value, mask):
        for b in range(bits):
            if mask >> b & 1:
                value = value + (1 << b) - (2 << b) * lax.rem(lax.div(value, 1 << b), 2)
        return value

    barrier = pltpu.get_barrier_semaphore()

    def greet(k, carry):
        pl.semaphore_signal(
            barrier, inc=1, device_id={"fsdp": lax.rem(me + k, n)}, device_id_type=MESH
        )
        return carry

    lax.fori_loop(1, n, greet, 0)
    for b in range(bits):
        pl.semaphore_signal(
            barrier, inc=1, device_id={"dom": flip(dom, 1 << b)}, device_id_type=MESH
        )

    def cols(j):
        return pl.ds(pl.multiple_of(j * cw, cw), cw)

    def depth_cols(pc):
        return pl.ds(pl.multiple_of(pc * pw, pw), pw)

    def chip_rows(chip):
        return pl.ds(pl.multiple_of(chip * (2 * rows), 2 * rows), 2 * rows)

    def core_rows(chip, core):
        return pl.ds(pl.multiple_of((chip * 2 + core) * rows, rows), rows)

    def sw_load(j):
        return pltpu.make_async_copy(sw_ref.at[:, cols(j)], dom_out.at[:, cols(j)], sw_sem.at[j])

    def dw_load(j):
        return pltpu.make_async_copy(dw_ref.at[:, cols(j)], tb.at[j], dw_sem.at[j])

    own_x = pltpu.make_async_copy(x_ref, xs.at[core_rows(z, c)], own_sem.at[0])
    own_g = pltpu.make_async_copy(
        g_ref.at[:, pl.ds(pl.multiple_of(me * width, width), width)],
        gs.at[core_rows(z, c)],
        own_sem.at[1],
    )
    for j in range(CHUNKS):
        sw_load(j).start()
        dw_load(j).start()
    own_x.start()
    own_g.start()

    pl.semaphore_wait(barrier, n - 1 + bits)

    part = rows // HALVES

    def x_slot(chip, core, h):
        at = (chip * 2 + core) * rows + h * part
        return xs.at[pl.ds(pl.multiple_of(at, part), part)]

    def x_copy(src, chip, core, h, sem, target):
        return pltpu.make_async_remote_copy(
            src_ref=src,
            dst_ref=x_slot(chip, core, h),
            send_sem=sem.at[chip, h],
            recv_sem=x_sem.at[chip * 2 + core, h],
            device_id={"fsdp": target},
            device_id_type=MESH,
        )

    def g_copy(target, j):
        at = pl.ds(pl.multiple_of(target * width + j * cw, cw), cw)
        return pltpu.make_async_remote_copy(
            src_ref=g_ref.at[:, at],
            dst_ref=gs.at[core_rows(z, c), cols(j)],
            send_sem=gsend_sem.at[target, j],
            recv_sem=g_sem.at[me, j],
            device_id={"fsdp": target},
            device_id_type=MESH,
        )

    for h in range(HALVES):
        mine = x_ref.at[pl.ds(h * part, part)]

        @pl.when(z + 1 < nz)
        def _():
            x_copy(mine, z, c, h, up_sem, up).start()

        @pl.when(z > 0)
        def _():
            x_copy(mine, z, c, h, down_sem, down).start()

        x_copy(mine, z, c, h, side_sem, sibling).start()

    def each_chunk(body):
        def step(j, carry):
            body(j)
            return carry

        lax.fori_loop(0, CHUNKS, step, 0)

    each_chunk(lambda j: g_copy(sibling, j).start())

    def send_g_near(chip):
        def one(j):
            for core in range(2):
                g_copy(chip * 2 + core, j).start()

        each_chunk(one)

    def is_end(chip):
        return (chip == 0) | (chip == nz - 1)

    def is_far(chip):
        return (chip >= 0) & (chip < nz) & ((chip > z + 1) | (chip < z - 1))

    def send_g_middle(j):
        def one(chip, carry):
            @pl.when(is_far(chip))
            def _():
                for core in range(2):
                    g_copy(chip * 2 + core, j).start()

            return carry

        lax.fori_loop(1, nz - 1, one, 0)

    def send_g_end(level):
        for chip in (0, nz - 1):
            across = is_end(z)
            mine = jnp.logical_not(across) if level == 2 else True

            @pl.when(is_far(chip) & mine)
            def _():
                pl.semaphore_wait(ready.at[level, chip], 2)

                def one(j, carry):
                    for core in range(2):
                        g_copy(chip * 2 + core, j).start()
                    return carry

                until = (1, jnp.where(across, CHUNKS, 2), CHUNKS)[level]
                lax.fori_loop(level, until, one, 0)

    def tell_far(level):
        def one(chip, carry):
            theirs = jnp.logical_not(is_end(chip)) if level == 2 else True

            @pl.when(is_far(chip) & theirs)
            def _():
                for core in range(2):
                    pl.semaphore_signal(
                        ready.at[level, z],
                        inc=1,
                        device_id={"fsdp": chip * 2 + core},
                        device_id_type=MESH,
                    )

            return carry

        @pl.when(is_end(z))
        def _():
            lax.fori_loop(0, nz, one, 0)

    et = min(512, depth)

    def make_weff(j):
        sw_load(j).wait()
        dw_load(j).wait()

        def one(i, carry):
            at = pl.ds(pl.multiple_of(i * et, et), et)
            weff[at, cols(j)] = (
                dom_out[at, cols(j)].astype(F32) * tb[j, at, :].astype(F32)
            ).astype(BF16)
            return carry

        lax.fori_loop(0, depth // et, one, 0)

    each_chunk(make_weff)
    own_x.wait()
    own_g.wait()

    count = count_ref[0]
    scale = lax.rsqrt(jnp.full((1, 1), count, jnp.int32).astype(F32))

    def wait_x_half(chip, core, h):
        slot = x_slot(chip, core, h)
        x_copy(slot, chip, core, h, side_sem, sibling).wait_recv()

    def wait_x(chip, core):
        for h in range(HALVES):
            wait_x_half(chip, core, h)

    def wait_g(chip, core, j):
        pltpu.make_async_remote_copy(
            src_ref=gs.at[core_rows(chip, core), cols(j)],
            dst_ref=gs.at[core_rows(chip, core), cols(j)],
            send_sem=gsend_sem.at[me, j],
            recv_sem=g_sem.at[chip * 2 + core, j],
            device_id={"fsdp": sibling},
            device_id_type=MESH,
        ).wait_recv()

    def pre(chip, j):
        here = chip_rows(chip)
        preact = jnp.dot(xs[here, :], weff[:, cols(j)], preferred_element_type=F32)
        sigma = jax.nn.sigmoid(preact)
        wait_g(chip, 1 - c, j)

        @pl.when(chip != z)
        def _():
            wait_g(chip, c, j)

        position = chip * (2 * rows) + lax.broadcasted_iota(jnp.int32, preact.shape, 0)
        slope = gs[here, cols(j)].astype(F32) * sigma * (1.0 + preact * (1.0 - sigma))
        gs[here, cols(j)] = jnp.where(position < count, slope, 0.0).astype(BF16)

    def sib_copy(chip, slot, pc):
        return pltpu.make_async_remote_copy(
            src_ref=dxb.at[slot, pc, pl.ds(pl.multiple_of((1 - c) * rows, rows), rows)],
            dst_ref=sib.at[chip, pc],
            send_sem=sib_send.at[chip, pc],
            recv_sem=sib_recv.at[chip, pc],
            device_id={"fsdp": sibling},
            device_id_type=MESH,
        )

    def chain_copy(slot, chip, pc, target):
        return pltpu.make_async_remote_copy(
            src_ref=sib.at[chip, pc],
            dst_ref=chain.at[slot, pc],
            send_sem=ch_send.at[chip, pc],
            recv_sem=ch_recv.at[slot, pc],
            device_id={"fsdp": target},
            device_id_type=MESH,
        )

    def send_up(chip, pc):
        return chain_copy(chip, chip, pc, lax.rem(me + 2, n))

    def send_down(chip, pc):
        return chain_copy(jnp.where(chip == z - 1, nz, chip), chip, pc, lax.rem(me + n - 2, n))

    def pair_sum(chip, slot, pc):
        sib_copy(chip, slot, pc).wait_send()
        sib_copy(chip, slot, pc).wait_recv()
        own = dxb[slot, pc, pl.ds(pl.multiple_of(c * rows, rows), rows), :]
        sib[chip, pc] = (own.astype(F32) + sib[chip, pc].astype(F32)).astype(BF16)

        @pl.when((z == 0) & (chip > z))
        def _():
            send_up(chip, pc).start()

        @pl.when((z == nz - 1) & (chip < z))
        def _():
            send_down(chip, pc).start()

    def each_piece(body):
        def step(pc, carry):
            body(pc)
            return carry

        lax.fori_loop(0, PIECES, step, 0)

    def back(chip, turn, before, pending):
        slot = lax.rem(turn, 2)

        def one(group, carry):
            wide = PAIR * pw
            at = pl.ds(pl.multiple_of(group * wide, wide), wide)
            partial = lax.dot_general(
                gs[chip_rows(chip), :],
                weff[at, :],
                (((1,), (1,)), ((), ())),
                preferred_element_type=F32,
            ).astype(BF16)
            for i in range(PAIR):
                pc = group * PAIR + i
                dxb[slot, pc] = partial[:, i * pw : (i + 1) * pw]
                sib_copy(chip, slot, pc).start()

            @pl.when(pending)
            def _():
                for i in range(PAIR):
                    pair_sum(before, 1 - slot, group * PAIR + i)

            return carry

        lax.fori_loop(0, PIECES // PAIR, one, 0)

    wait_x(z, 1 - c)
    each_chunk(lambda j: pre(z, j))
    back(z, 0, z, False)

    def receive(chip, h, forward, target, sem):
        wait_x_half(chip, c, h)
        slot = x_slot(chip, c, h)

        @pl.when(forward)
        def _():
            x_copy(slot, chip, c, h, sem, target).start()

        x_copy(slot, chip, c, h, side_sem, sibling).start()

    def receive_both(distance, h):
        below, above = z - distance, z + distance

        @pl.when(below >= 0)
        def _():
            receive(below, h, z + 1 < nz, up, up_sem)

        @pl.when(above < nz)
        def _():
            receive(above, h, z > 0, down, down_sem)

    @pl.when(z == 0)
    def _():
        send_g_near(z + 1)

    @pl.when(z == nz - 1)
    def _():
        send_g_near(z - 1)

    def gather_step(distance, carry):
        for h in range(HALVES):
            receive_both(distance, h)

        @pl.when((distance == 1) & (z > 0) & (z < nz - 1))
        def _():
            send_g_near(z + 1)
            send_g_near(z - 1)

        @pl.when(distance == nz - 2)
        def _():
            each_chunk(send_g_middle)

        return carry

    lax.fori_loop(1, nz - 1, gather_step, 0)

    def near(side, carry):
        turn, before = carry
        chip = z - 1 + 2 * side
        valid = (chip >= 0) & (chip < nz)

        @pl.when(valid)
        def _():
            wait_x(chip, 1 - c)
            each_chunk(lambda j: pre(chip, j))
            back(chip, turn, before, True)

        return jnp.where(valid, turn + 1, turn), jnp.where(valid, chip, before)

    turns, last = lax.fori_loop(0, 2, near, (1, z))

    def flush(chip, turn, first, last):
        def one(pc, carry):
            pair_sum(chip, lax.rem(turn, 2), pc)
            return carry

        lax.fori_loop(first, last, one, 0)

    flush(last, turns - 1, 0, PIECES // 4)
    for h in range(HALVES):
        receive_both(nz - 1, h)
        if h == 0:
            tell_far(0)
            send_g_end(0)
            flush(last, turns - 1, PIECES // 4, PIECES)
    tell_far(1)

    @pl.when(is_end(z))
    def _():
        send_g_end(1)

    farthest = jnp.where(z < nz // 2, nz - 1, 0)

    def each_far(body):
        def one(k, carry):
            chip = jnp.where(z < nz // 2, nz - 1 - k, k)
            return body(chip, is_far(chip), carry)

        return lambda carry: lax.fori_loop(0, nz, one, carry)

    order = sorted(range(nd), key=lambda m: (-bin(m).count("1"), m))

    def bit_order(p):
        return [(p + s) % bits for s in range(bits)]

    def sent_at(m, p):
        return next((s for s, b in enumerate(bit_order(p)) if m >> b & 1), bits)

    index = [{} for _ in range(parts)]
    for p in range(parts):
        for m in range(1, nd):
            s = sent_at(m, p)
            index[p][s, m ^ (1 << bit_order(p)[s])] = len(index[p])

    def tile_rows(m, q):
        return pl.ds(pl.multiple_of(flip(dom, m) * block + q * tile, tile), tile)

    def block_rows(m):
        return pl.ds(pl.multiple_of(flip(dom, m) * block, block), block)

    def d_copy(j, m, q):
        p = q % parts
        s = sent_at(m, p)
        bit = 1 << bit_order(p)[s]
        at = index[p][s, m ^ bit]
        return pltpu.make_async_remote_copy(
            src_ref=tb.at[j, tile_rows(m, q)],
            dst_ref=rb.at[at, j, pl.ds(q * tile, tile)],
            send_sem=d_send.at[at, j, q],
            recv_sem=d_recv.at[at, j, q],
            device_id={"dom": flip(dom, bit)},
            device_id_type=MESH,
        )

    def arrived(j, m, q, steps):
        p = q % parts
        total = tb[j, tile_rows(m, q), :].astype(F32)
        for s in range(steps):
            at = index[p][s, m]
            here = pl.ds(q * tile, tile)
            pltpu.make_async_remote_copy(
                src_ref=rb.at[at, j, here],
                dst_ref=rb.at[at, j, here],
                send_sem=d_send.at[at, j, q],
                recv_sem=d_recv.at[at, j, q],
                device_id={"dom": flip(dom, 1 << bit_order(p)[s])},
                device_id_type=MESH,
            ).wait_recv()
            total = total + rb[at, j, here, :].astype(F32)
        return total

    def weight_chunk(j):
        for m in order:
            at = block_rows(m)
            scaled = scale * lax.dot_general(
                xs[:, at], gs[:, cols(j)], (((0,), (0,)), ((), ())), preferred_element_type=F32
            )
            tb[j, at, :] = (scaled * tb[j, at, :].astype(F32)).astype(BF16)
            for q in range(pieces):
                if sent_at(m, q % parts) == 0:
                    d_copy(j, m, q).start()
            dom_out[at, cols(j)] = (scaled * dom_out[at, cols(j)].astype(F32)).astype(BF16)

    def wait_far_x(chip, valid, carry):
        @pl.when(valid)
        def _():
            wait_x(chip, 1 - c)

        return carry

    each_far(wait_far_x)(0)

    def chunk_step(j):
        @pl.when((j == 1) & (z > 0) & (z < nz - 1))
        def _():
            send_g_end(1)

        @pl.when((j == 2) & (z > 0) & (z < nz - 1))
        def _():
            send_g_end(2)

        @pl.when(j <= EARLY)
        def _():
            def some(i, carry):
                pre(farthest, i)
                return carry

            lax.fori_loop(j, jnp.where(j == EARLY, CHUNKS, j + 1), some, 0)

        @pl.when(j == 0)
        def _():
            tell_far(2)

        @pl.when(j == EARLY)
        def _():
            back(farthest, turns, farthest, False)
            flush(farthest, turns, 0, PIECES)

        def far_pre(chip, valid, carry):
            @pl.when(valid & (chip != farthest))
            def _():
                pre(chip, j)

            return carry

        each_far(far_pre)(0)

        @pl.when(j == CHUNKS - 1)
        def _():
            def far_back(chip, valid, carry):
                turn, before, pending = carry
                new = valid & (chip != farthest)

                @pl.when(new)
                def _():
                    back(chip, turn, before, pending > 0)

                return (
                    jnp.where(new, turn + 1, turn),
                    jnp.where(new, chip, before),
                    jnp.where(new, 1, pending),
                )

            turn, before, pending = each_far(far_back)((turns + 1, farthest, 0))

            @pl.when(pending > 0)
            def _():
                flush(before, turn - 1, 0, PIECES)

        weight_chunk(j)

    each_chunk(chunk_step)

    hops = (nz - 1) * PIECES

    def take(slot, chip, pc):
        pltpu.make_async_remote_copy(
            src_ref=chain.at[slot, pc],
            dst_ref=chain.at[slot, pc],
            send_sem=ch_send.at[chip, pc],
            recv_sem=ch_recv.at[slot, pc],
            device_id={"fsdp": sibling},
            device_id_type=MESH,
        ).wait_recv()
        sib[chip, pc] = (sib[chip, pc].astype(F32) + chain[slot, pc].astype(F32)).astype(BF16)

    def turn_of(step):
        turn = lax.div(step, PIECES)
        rising = jnp.where(turn == 0, 1, nz - turn)
        return rising, lax.rem(step, PIECES), (step >= 0) & (step < hops)

    def hop(t):
        rising, pc, valid = turn_of(t - LAG * (z - 1))

        @pl.when(valid & (z > 0) & (rising >= z))
        def _():
            take(rising, rising, pc)

            @pl.when(rising > z)
            def _():
                send_up(rising, pc).start()

        mirrored, pd, due = turn_of(t - LAG * (nz - 2 - z))
        falling = nz - 1 - mirrored

        @pl.when(due & (z < nz - 1) & (falling <= z))
        def _():
            take(jnp.where(falling == z, nz, falling), falling, pd)

            @pl.when(falling < z)
            def _():
                send_down(falling, pd).start()

    def relay(j):
        for s in range(1, bits):
            for m in order:
                for q in range(pieces):
                    if m and sent_at(m, q % parts) == s:
                        total = arrived(j, m, q, s).astype(BF16)
                        tb[j, tile_rows(m, q), :] = total
                        d_copy(j, m, q).start()

    spread = PIECES // 2

    def tail_step(t, carry):
        hop(t)
        mark = t - (PIECES - 1)

        @pl.when((mark >= 0) & (lax.rem(mark, spread) == 0) & (mark < spread * CHUNKS))
        def _():
            relay(lax.div(mark, spread))

        return carry

    lax.fori_loop(0, max(hops + LAG * (nz - 2), PIECES - 1 + spread * CHUNKS), tail_step, 0)

    for pc in range(PIECES):
        in_out[:, pc * pw : (pc + 1) * pw] = sib[z, pc]

    def final(j):
        for q in range(pieces):
            shared_out[pl.ds(q * tile, tile), cols(j)] = arrived(j, 0, q, bits)

    each_chunk(final)

    def drain_chip(chip, carry):
        for h in range(HALVES):
            slot = x_slot(chip, c, h)

            @pl.when((chip <= z) & (z + 1 < nz))
            def _():
                x_copy(slot, chip, c, h, up_sem, up).wait_send()

            @pl.when((chip >= z) & (z > 0))
            def _():
                x_copy(slot, chip, c, h, down_sem, down).wait_send()

            x_copy(slot, chip, c, h, side_sem, sibling).wait_send()

        def sums(pc):
            @pl.when(chip > z)
            def _():
                send_up(chip, pc).wait_send()

            @pl.when(chip < z)
            def _():
                send_down(chip, pc).wait_send()

        each_piece(sums)
        return carry

    lax.fori_loop(0, nz, drain_chip, 0)

    def drain_g(k, carry):
        each_chunk(lambda j: g_copy(lax.rem(me + k, n), j).wait_send())
        return carry

    lax.fori_loop(1, n, drain_g, 0)

    def drain_d(j):
        for m in range(1, nd):
            for q in range(pieces):
                d_copy(j, m, q).wait_send()

    each_chunk(drain_d)


def fused(n, nd, x, g, sw, dw, count):
    rows, depth = x.shape
    width = sw.shape[1]
    nz = n // 2
    total = n * rows
    block = depth // nd
    bits = nd.bit_length() - 1
    tile = min(TILE, block // min(2, bits))
    pieces = block // tile
    cw, pw = width // CHUNKS, depth // PIECES
    kept = block * width * 4 + depth * width * 2 + rows * depth * 2
    any_spec = pl.BlockSpec(memory_space=pl.ANY)
    dma = pltpu.SemaphoreType.DMA
    vmem = pltpu.VMEM
    return pl.pallas_call(
        functools.partial(fused_kernel, n, nd),
        out_shape=(
            vmem((block, width), F32),
            vmem((depth, width), BF16),
            vmem((rows, depth), BF16),
        ),
        in_specs=[any_spec] * 4 + [pl.BlockSpec(memory_space=pltpu.SMEM)],
        out_specs=(pl.BlockSpec(memory_space=vmem),) * 3,
        scratch_shapes=[
            vmem((total, depth), BF16),
            vmem((total, width), BF16),
            vmem((depth, width), BF16),
            vmem((CHUNKS, depth, cw), BF16),
            vmem((nd - 1, CHUNKS, block, cw), BF16),
            vmem((nz, PIECES, rows, pw), BF16),
            vmem((nz + 1, PIECES, rows, pw), BF16),
            vmem((2, PIECES, 2 * rows, pw), BF16),
            dma((nz, HALVES)),
            dma((nz, HALVES)),
            dma((nz, HALVES)),
            dma((n, HALVES)),
            dma((n, CHUNKS)),
            dma((n, CHUNKS)),
            dma((2,)),
            dma((CHUNKS,)),
            dma((CHUNKS,)),
            dma((nz, PIECES)),
            dma((nz, PIECES)),
            dma((nz, PIECES)),
            dma((nz + 1, PIECES)),
            dma((nd - 1, CHUNKS, pieces)),
            dma((nd - 1, CHUNKS, pieces)),
            pltpu.SemaphoreType.REGULAR((3, nz)),
        ],
        compiler_params=pltpu.CompilerParams(
            collective_id=0, has_side_effects=True, vmem_limit_bytes=LIMIT - kept
        ),
        name="gather_backprop_reduce",
    )(x, g, sw, dw, count)


def store_kernel(count, *refs):
    sources, targets, sem = refs[:count], refs[count : 2 * count], refs[2 * count]
    copies = []
    for i in range(count):
        step = sources[i].shape[0] // STORES
        for k in range(STORES):
            at = pl.ds(k * step, step)
            copies.append(pltpu.make_async_copy(sources[i].at[at], targets[i].at[at], sem.at[i, k]))
    for copy in copies:
        copy.start()
    for copy in copies:
        copy.wait()


def store_results(*arrays):
    count = len(arrays)
    return pl.pallas_call(
        functools.partial(store_kernel, count),
        out_shape=tuple(jax.ShapeDtypeStruct(a.shape, a.dtype) for a in arrays),
        in_specs=[pl.BlockSpec(memory_space=pltpu.VMEM)] * count,
        out_specs=(pl.BlockSpec(memory_space=pl.ANY),) * count,
        scratch_shapes=[pltpu.SemaphoreType.DMA((count, STORES))],
        compiler_params=pltpu.CompilerParams(vmem_limit_bytes=16 * 1024 * 1024),
        name="store_results",
    )(*arrays)


def solution(mesh):
    n, nd = mesh.shape["fsdp"], mesh.shape["dom"]

    def body(inputs, cotangent, shared_weight, domain_weight, row_counts):
        results = fused(
            n, nd, inputs[0], cotangent[0], shared_weight, domain_weight[0], row_counts
        )
        results = [pltpu.with_memory_space_constraint(a, pltpu.VMEM) for a in results]
        shared_grad, domain_grad, input_grad = store_results(*results)
        return (shared_grad, domain_grad[None], input_grad[None])

    return jax.shard_map(
        body,
        mesh=mesh,
        in_specs=(
            P("dom", "fsdp", None),
            P("dom", "fsdp", None),
            P(None, "fsdp"),
            P("dom", None, "fsdp"),
            P("dom"),
        ),
        out_specs=(P("dom", "fsdp"), P("dom", None, "fsdp"), P("dom", "fsdp", None)),
        check_vma=False,
    )
```
